32 devices in a mesh: segment: 4 (over y, x), dom: 8 (over z, core).
Axes of the slice: x: 2, y: 2, z: 4, core: 2. Of those that a mesh axis runs over, the one named last changes fastest.
Arguments:
- samples: bfloat16 [4, 4096, 512], P(None, 'dom'), may hold values from -6 to 6
- w_source: bfloat16 [4, 1, 512, 512], P('segment'), may hold values from -0.25 to 0.25
- w_self: bfloat16 [4, 1, 512, 512], P('segment'), may hold values from -0.25 to 0.25
- w_message: bfloat16 [4, 1, 512, 512], P('segment'), may hold values from -0.25 to 0.25
- w_output: bfloat16 [4, 1, 512, 512], P('segment'), may hold values from -0.25 to 0.25
- norm_gain: float32 [4, 1, 512], P('segment'), may hold values from 0.1 to 1.9
- tile_source: int32 [4, 32, 6], P('segment', 'dom'), may hold values from 0 to 31, as said below
- tile_count: int32 [4, 32], P('segment', 'dom'), may hold values from 3 to 6, as said below
- tile_value: bfloat16 [4, 32, 6, 128, 128], P('segment', 'dom'), may hold values from -0.21875 to 0.21875
Outputs:
- final: bfloat16 [4, 4096, 512], P('segment', 'dom')
The draws below stay inside these ranges and needn't reach their ends.
Inputs may be any that keep to these rules, and one draw needn't show every extreme that they name: `tile_source`: each entry for destination block b names a block among the 4 blocks that hold b's dom index (blocks (b // 4) * 4 .. + 4 - 1) or the 1 block on either side of them, counted cyclically over 32. `tile_count`: slots at or beyond the count are unused; the first block of every dom index uses all 6 slots.
All inputs are finite; a program needn't handle non-finite values.
Results may differ from the reference program's by a relative error of at most 0.013.
Values may be sent and summed in bfloat16 or wider, within the bound.
A program may use at most 64 MiB of HBM per device.

```python
import jax
import jax.numpy as jnp
from jax import lax

D = 512
BLK = 128
BD = 4
HB = 1
K = 6
LPS = 1
SAMPLES = 4
SEGMENTS = 4
NBLK = 32
NODES = 4096


def draw_tile_source(key, part):
    blocks = jnp.arange(NBLK, dtype=jnp.int32)
    base = blocks // BD * BD - HB
    offsets = jax.random.randint(jax.random.fold_in(key, 11), (SEGMENTS, NBLK, K), 0, BD + 2 * HB)
    lower = jax.random.randint(jax.random.fold_in(key, 12), (SEGMENTS, NBLK), 0, HB)
    upper = jax.random.randint(jax.random.fold_in(key, 13), (SEGMENTS, NBLK), BD + HB, BD + 2 * HB)
    own = jnp.broadcast_to(blocks % BD + HB, (SEGMENTS, NBLK))
    offsets = offsets.at[:, :, 0].set(own)
    offsets = offsets.at[:, :, 1].set(lower)
    offsets = offsets.at[:, :, 2].set(upper)
    return jnp.mod(base[None, :, None] + offsets, NBLK).astype(jnp.int32)


def draw_tile_count(key, part):
    counts = jax.random.randint(jax.random.fold_in(key, 21), (SEGMENTS, NBLK), 3, K + 1)
    first = (jnp.arange(NBLK, dtype=jnp.int32) % BD == 0)[None, :]
    return jnp.where(first, K, counts).astype(jnp.int32)


def steps_of(key, dims, shards, low, largest):
    def one(axis_at, shards_of):
        steps = jax.random.uniform(jax.random.fold_in(jax.random.fold_in(key, 6), axis_at), (shards_of,), jnp.float32, low / len(shards), largest / len(shards))
        return jnp.repeat(jnp.exp(steps), dims[axis_at] // shards_of).reshape((-1,) + (1,) * (len(dims) - axis_at - 1))

    gain = one(*shards[0])
    for cut in shards[1:]:
        gain = gain * one(*cut)
    return gain


def noise(stream_key, dims, width, limit, split=(), kind=jnp.bfloat16):
    entries = jax.random.normal(stream_key, dims, jnp.float32) * width
    if len(split) > 0:
        entries = steps_of(stream_key, dims, split, -0.22, 0.18) * entries
    return jnp.clip(entries, min=-limit, max=limit).astype(kind)


def setup_inputs(seed: int = 0) -> dict:
    arg_keys = jax.random.split(jax.random.key(seed), 10)
    samples = noise(arg_keys[0], (SAMPLES, NODES, D), 1.0, 6.0, ((1, 8),))
    w_source = noise(arg_keys[1], (SEGMENTS, LPS, D, D), D ** -0.5, 0.25, ((0, 4),))
    w_self = noise(arg_keys[2], (SEGMENTS, LPS, D, D), D ** -0.5, 0.25, ((0, 4),))
    w_message = noise(arg_keys[3], (SEGMENTS, LPS, D, D), D ** -0.5, 0.25, ((0, 4),))
    w_output = noise(arg_keys[4], (SEGMENTS, LPS, D, D), D ** -0.5, 0.25, ((0, 4),))
    norm_gain = jnp.clip(1.0 + 0.18 * jax.random.normal(arg_keys[5], (SEGMENTS, LPS, D), jnp.float32), 0.1, 1.9)
    tile_source = draw_tile_source(jax.random.fold_in(arg_keys[9], 71), 0)
    tile_count = draw_tile_count(jax.random.fold_in(arg_keys[9], 71), 0)
    tile_value = noise(arg_keys[8], (SEGMENTS, NBLK, K, BLK, BLK), (BLK * K) ** -0.5, 0.21875, ((0, 4), (1, 8)))
    return dict(samples=samples, w_source=w_source, w_self=w_self, w_message=w_message, w_output=w_output, norm_gain=norm_gain, tile_source=tile_source, tile_count=tile_count, tile_value=tile_value)


def run_layer(h, w_source, w_self, w_message, w_output, norm_gain, sources, counts, tiles):
    sender = jax.nn.silu(jnp.dot(h, w_source, preferred_element_type=jnp.float32)).astype(jnp.bfloat16)
    sender_blocks = sender.reshape(NBLK, BLK, D)
    slots = jnp.arange(K, dtype=jnp.int32)

    def one_block(packed):
        src_row, count_one, tile_set = packed
        keep = (slots < count_one).astype(jnp.float32)
        weights = tile_set.astype(jnp.float32) * keep[:, None, None]
        picked = sender_blocks[src_row.astype(jnp.int32)].astype(jnp.float32)
        return jnp.einsum('kij,kjd->id', weights, picked)
    gathered = lax.map(one_block, (sources, counts, tiles)).reshape(NODES, D).astype(jnp.bfloat16)
    mixed = jnp.dot(h, w_self, preferred_element_type=jnp.float32) + jnp.dot(gathered, w_message, preferred_element_type=jnp.float32)
    scaled = mixed / jnp.sqrt(lax.optimization_barrier(jnp.mean(mixed * mixed, axis=-1, keepdims=True)) + 1e-05) * norm_gain
    update = jax.nn.silu(scaled).astype(jnp.bfloat16)
    return (h.astype(jnp.float32) + jnp.dot(update, w_output, preferred_element_type=jnp.float32)).astype(jnp.bfloat16)

def reference(samples, w_source, w_self, w_message, w_output, norm_gain, tile_source, tile_count, tile_value):
    outputs = []
    for sample in range(SAMPLES):
        h = samples[sample]
        for section in range(SEGMENTS):
            for layer in range(LPS):
                h = run_layer(h, w_source[section, layer], w_self[section, layer], w_message[section, layer], w_output[section, layer], norm_gain[section, layer], tile_source[section], tile_count[section], tile_value[section])
        outputs.append(h)
    return jnp.stack(outputs)
```

```python
import functools

import jax
import jax.numpy as jnp
from jax import lax
from jax.experimental import pallas as pl
from jax.experimental.pallas import tpu as pltpu
from jax.sharding import PartitionSpec as P

HB = 1
MESH = pl.DeviceIdType.MESH
MATS = 4

WEIGHT_TIMES = {
    (0, 1): (3.8, 6.5, 9.3, 12.0),
    (0, 2): (3.8, 6.5, 9.3, 12.0),
    (0, 3): (31.3, 34.0, 36.8, 39.5),
    (1, 2): (9.3, 14.8, 20.3, 23.0),
    (1, 3): (3.8, 6.5, 12.0, 17.5),
    (2, 1): (9.3, 14.8, 20.3, 23.0),
    (2, 3): (3.8, 6.5, 12.0, 17.5),
    (3, 1): (3.8, 6.5, 9.3, 12.0),
    (3, 2): (3.8, 6.5, 9.3, 12.0),
}
EDGE_TIMES = {
    (0, 1): (16.0, 20.0, 24.1, 28.3),
    (0, 2): (16.0, 20.0, 24.1, 28.3),
    (0, 3): (43.6, 32.3, 36.4, 40.5),
    (1, 2): (28.0, 32.0, 36.0, 40.0),
    (1, 3): (27.0, 31.2, 35.3, 39.5),
    (2, 1): (25.0, 29.0, 33.0, 37.0),
    (2, 3): (39.5, 27.0, 31.2, 35.3),
    (3, 1): (16.0, 25.7, 29.8, 34.0),
    (3, 2): (16.0, 25.7, 29.8, 34.0),
}
STATE_TIMES = {1: 24.0, 2: 20.0, 3: 21.6}
RELAY_TIME = 11.0
PIECES = 4
PIECE_TIMES = (0.9, 0.6, 1.2, 1.2)


def edge_target(role, section, block):
    if role == 0 and section in (1, 2):
        return 3 - section
    if role == 1 and section == 3 and block == 0:
        return 0
    if role == 2 and section == 3 and block > 0:
        return 0
    return None


def weight_target(role, section):
    if role == 3:
        return 3 - section
    if role == 1 and section == 3:
        return 0
    return None


def order_of(role, sections, blocks):
    events = []
    for s in range(1, sections):
        if s == role:
            continue
        for j, t in enumerate(WEIGHT_TIMES[role, s]):
            events.append((t, ("x", s, j)))
            events.append((t + 4.2, ("z", s, j)))
        for b in range(blocks):
            if edge_target(role, s, b) is not None:
                events.append((EDGE_TIMES[role, s][b], ("e", s, b)))
    if role in (1, 2):
        events.append((RELAY_TIME, ("r", 0, 0)))
    events.sort()
    times = {key: t for t, key in events}
    buckets = {}
    now = 1.0
    half = blocks // 2
    for u in range(2 * sections - 1):
        if u < sections and role != 0:
            continue
        s = max(u - sections + 1, 0)
        for p in range(PIECES):
            needs = []
            ready = now
            if s != role:
                mats = ((0,), (1,), (2, 3), ())[p]
                for j in mats:
                    needs += [("x", s, j), ("z", s, j)]
                    ready = max(ready, WEIGHT_TIMES[role, s][j] + 5.5)
                if p >= 2:
                    for b in range((p - 2) * half, (p - 1) * half):
                        ready = max(ready, EDGE_TIMES[role, s][b])
                        if ("e", s, b) in times:
                            needs.append(("e", s, b))
            if u == sections and p == 0 and role != 0:
                ready = max(ready, STATE_TIMES[role])
            chosen = [e for e in events if e[0] <= ready or e[1] in needs]
            if chosen:
                last = max(e[0] for e in chosen)
                chosen = [e for e in events if e[0] <= last]
                ready = max(ready, last)
            events = [e for e in events if e not in chosen]
            buckets[u, p] = [key for _, key in chosen]
            now = ready + PIECE_TIMES[p]
    buckets["end"] = [key for _, key in events]
    return buckets


def silu(v):
    half = 0.5 * v
    return half + half * jnp.tanh(half)


def kernel(
    sections, domains,
    source_ref, count_ref, samples_ref, wa_ref, wb_ref, wc_ref, wd_ref, gain_ref, tiles_ref,
    out_ref,
    W, E, G, T, H, PAD, BASE,
    l_sem, rx, rz, rc, rg, ra, rr, rh, sx, sf, sz, sc, sg, sa, sr, sh, so,
):
    g = lax.axis_index("segment")
    d = lax.axis_index("dom")
    w_refs = (wa_ref, wb_ref, wc_ref, wd_ref)
    _, blocks, slots, blk, _ = tiles_ref.shape
    window = blocks + 2 * HB
    rows = blocks * blk
    halo = HB * blk
    width = samples_ref.shape[-1]
    quarter = width // 4
    half = rows // 2
    per_half = blocks // 2
    units = 2 * sections - 1
    roles = range(sections)
    q = lax.rem(d, 4)
    zd = d + 2 - 4 * (q // 2)
    cd = d + 1 - 2 * lax.rem(d, 2)
    nxt, prv = lax.rem(d + 1, domains), lax.rem(d + domains - 1, domains)
    zq = lax.rem(zd, 4)
    cq = lax.rem(cd, 4)
    czq = lax.rem(q + 1 - 2 * lax.rem(q, 2) + 2, 4)

    def part(index):
        return pl.ds(pl.multiple_of(index * quarter, quarter), quarter)

    def remote(src, dst, send, recv, device):
        return pltpu.make_async_remote_copy(
            src_ref=src, dst_ref=dst, send_sem=send, recv_sem=recv,
            device_id=device, device_id_type=MESH,
        )

    def piece_of(s, j):
        if j < MATS:
            return W.at[s, j, part(q)]
        return E.at[s, pl.ds((j - MATS) * blk, blk)]

    def own(role, side, j):
        src = w_refs[j].at[0, 0, part(q)] if j < MATS else piece_of(role, j)
        to = role ^ (1 + side)
        return remote(src, piece_of(role, j), sx.at[side, j], rx.at[role, j], (to, d))

    def forward(s, j, to):
        return remote(piece_of(s, j), piece_of(s, j), sf.at[s, j], rx.at[s, j], (to, d))

    def to_pair(s, j):
        return remote(W.at[s, j, part(q)], W.at[s, j, part(q)], sz.at[s, j], rz.at[s, j], (g, zd))

    def to_core(s, j, kind):
        at = part(zq if kind else q)
        return remote(W.at[s, j, at], W.at[s, j, at], sc.at[s, j, kind], rc.at[s, j, kind], (g, cd))

    def wait_pair(s, j):
        remote(W.at[s, j, part(zq)], W.at[s, j, part(zq)], sz.at[s, j], rz.at[s, j], (g, zd)).wait_recv()

    def wait_core(s, j):
        for kind, index in enumerate((cq, czq)):
            at = part(index)
            remote(W.at[s, j, at], W.at[s, j, at], sc.at[s, j, kind], rc.at[s, j, kind], (g, cd)).wait_recv()

    def wait_block(s, b):
        at = pl.ds(b * blk, blk)
        remote(E.at[s, at], E.at[s, at], sf.at[s, MATS + b], rx.at[s, MATS + b], (g, cd)).wait_recv()

    def gain(role, k):
        to = role ^ (1 + k)
        return remote(gain_ref.at[pl.ds(0, 1)], G.at[pl.ds(role, 1)], sg.at[k], rg.at[role], (to, d))

    def wait_gain(s):
        remote(gain_ref.at[pl.ds(0, 1)], G.at[pl.ds(s, 1)], sg.at[0], rg.at[s], (g, cd)).wait_recv()

    def state(n, h):
        at = pl.ds(h * half, half)
        ref = H.at[n, at]
        last = sections - 1
        if n == last:
            return remote(ref, ref, sa.at[n, h], rr.at[0], (1 + h, d))
        return remote(ref, ref, sa.at[n, h], ra.at[h], (n, d))

    def relay(role):
        last = sections - 1
        ref = H.at[last, pl.ds((role - 1) * half, half)]
        return remote(ref, ref, sr.at[0], ra.at[role - 1], (last, d))

    def wait_state(n, h):
        ref = H.at[n, pl.ds(h * half, half)]
        remote(ref, ref, sr.at[0], ra.at[h], (g, cd)).wait_recv()

    def halos(u):
        first = PAD.at[u, pl.ds(halo, halo)]
        final = PAD.at[u, pl.ds(rows, halo)]
        return (
            remote(final, PAD.at[u, pl.ds(0, halo)], sh.at[u, 0], rh.at[u, 0], (g, nxt)),
            remote(first, PAD.at[u, pl.ds(halo + rows, halo)], sh.at[u, 1], rh.at[u, 1], (g, prv)),
        )

    def local_copies():
        made = [pltpu.make_async_copy(tiles_ref.at[0], T, l_sem.at[0])]
        made += [
            pltpu.make_async_copy(w_refs[j].at[0, 0], W.at[g, j], l_sem.at[1 + j]) for j in range(MATS)
        ]
        made.append(
            pltpu.make_async_copy(gain_ref.at[pl.ds(0, 1)], G.at[pl.ds(g, 1)], l_sem.at[1 + MATS])
        )
        return made

    samples_copy = pltpu.make_async_copy(samples_ref, H, l_sem.at[2 + MATS])

    for copy in local_copies():
        copy.start()

    @pl.when(g == 0)
    def _():
        samples_copy.start()

    barrier = pltpu.get_barrier_semaphore()
    peers = [(lax.rem(g + k, sections), d) for k in range(1, sections)]
    peers += [(g, zd), (g, cd), (g, nxt), (g, prv)]
    for peer in peers:
        pl.semaphore_signal(barrier, inc=1, device_id=peer, device_id_type=MESH)
    pl.semaphore_wait(barrier, len(peers))

    started = {role: [] for role in roles}

    def begin(role, make, *args):
        make(*args).start()
        started[role].append((make, args))

    for role in roles[1:]:
        @pl.when(g == role)
        def _():
            for j in range(MATS if role < 3 else 2):
                for side in range(2):
                    begin(role, own, role, side, j)
            for k in range(3):
                begin(role, gain, role, k)

    copies = local_copies()
    copies[0].wait()
    total = blocks * domains
    base = d * blocks - HB

    def densify(b, carry):
        local = [lax.rem(source_ref[0, b, k] - base + total, total) for k in range(slots)]
        count = count_ref[0, b]
        at = pl.ds(pl.multiple_of(b * blk, blk), blk)
        for w in range(window):
            summed = jnp.zeros((blk, blk), jnp.float32)
            for k in range(slots):
                keep = ((local[k] == w) & (count > k)).astype(jnp.float32)
                summed += T[b, k].astype(jnp.float32) * keep
            E[g, at, w * blk : (w + 1) * blk] = summed.astype(jnp.bfloat16)
        return carry

    lax.fori_loop(0, blocks, densify, 0)

    for role in (1, 2):
        @pl.when(g == role)
        def _():
            for b in range(blocks):
                begin(role, own, role, role - 1, MATS + b)
                if b == 0:
                    begin(role, own, role, 2 - role, MATS)

    for copy in copies[1:]:
        copy.wait()

    @pl.when(g == 0)
    def _():
        samples_copy.wait()

    def run(role, keys):
        for kind, s, j in keys:
            if kind == "x":
                forward(s, j, 0).wait_recv()
                begin(role, to_core, s, j, 0)
                begin(role, to_pair, s, j)
                to = weight_target(role, s)
                if to is not None:
                    begin(role, forward, s, j, to)
                if role == 3:
                    side = (to ^ role) - 1
                    if j < 2:
                        begin(role, own, role, side, j + 2)
                    if j == 3:
                        order = range(blocks)
                        if to == 2:
                            order = [*range(1, blocks), 0]
                        for b in order:
                            begin(role, own, role, side, MATS + b)
            elif kind == "z":
                wait_pair(s, j)
                begin(role, to_core, s, j, 1)
            elif kind == "e":
                wait_block(s, j)
                begin(role, forward, s, MATS + j, edge_target(role, s, j))
            else:
                ref = H.at[sections - 1, pl.ds((role - 1) * half, half)]
                remote(ref, ref, sr.at[0], rr.at[0], (g, cd)).wait_recv()
                begin(role, relay, role)
                for b in range(1, blocks):
                    begin(role, own, role, 2 - role, MATS + b)

    orders = {role: order_of(role, sections, blocks) for role in roles}

    def poll(u, p):
        for role in roles:
            for (unit, piece), keys in [kv for kv in orders[role].items() if kv[0] != "end"]:
                if piece == p and keys:
                    pl.when((g == role) & (u == unit))(functools.partial(run, role, keys))

    def unit_body(u, carry):
        s = jnp.maximum(u - (sections - 1), 0)
        n = jnp.where(u < sections, sections - 1 - u, g)
        active = (u >= sections) | (g == 0)
        fetched = s != g

        poll(u, 0)

        @pl.when(active)
        def _():
            @pl.when(fetched)
            def _():
                wait_core(s, 0)

            @pl.when((u == sections) & (g != 0))
            def _():
                for h in range(2):
                    wait_state(g, h)

            for i in range(2):
                at = pl.ds(i * half, half)
                v = jnp.dot(H[n, at], W[s, 0], preferred_element_type=jnp.float32)
                PAD[u, pl.ds(halo + i * half, half)] = silu(v).astype(jnp.bfloat16)
            for copy in halos(u):
                copy.start()

        poll(u, 1)

        @pl.when(active)
        def _():
            @pl.when(fetched)
            def _():
                wait_core(s, 1)

            for i in range(2):
                at = pl.ds(i * half, half)
                BASE[at] = jnp.dot(H[n, at], W[s, 1], preferred_element_type=jnp.float32)

        for i in range(2):
            poll(u, 2 + i)

            @pl.when(active)
            def _():
                @pl.when(fetched)
                def _():
                    if i == 0:
                        wait_core(s, 2)
                        wait_core(s, 3)
                        wait_gain(s)
                    for b in range(i * per_half, (i + 1) * per_half):
                        passed = jnp.bool_(False)
                        for role in roles:
                            for section in roles[1:]:
                                if section != role and edge_target(role, section, b) is not None:
                                    passed = passed | ((g == role) & (s == section))

                        @pl.when(jnp.logical_not(passed))
                        def _():
                            wait_block(s, b)

                if i == 0:
                    for copy in halos(u):
                        copy.wait_recv()
                at = pl.ds(i * half, half)
                gathered = jnp.dot(E[s, at], PAD[u], preferred_element_type=jnp.float32)
                mixed = BASE[at] + jnp.dot(
                    gathered.astype(jnp.bfloat16), W[s, 2], preferred_element_type=jnp.float32
                )
                scale = lax.rsqrt(jnp.mean(mixed * mixed, axis=-1, keepdims=True) + 1e-05)
                update = silu(mixed * scale * G[s]).astype(jnp.bfloat16)
                result = H[n, at].astype(jnp.float32) + jnp.dot(
                    update, W[s, 3], preferred_element_type=jnp.float32
                )
                H[n, at] = result.astype(jnp.bfloat16)

            for unit in range(sections - 1):
                @pl.when((g == 0) & (u == unit))
                def _():
                    begin(0, state, sections - 1 - unit, i)

            @pl.when(u == units - 1)
            def _():
                pltpu.make_async_copy(
                    H.at[g, pl.ds(i * half, half)], out_ref.at[0, pl.ds(i * half, half)], so.at[i]
                ).start()

        @pl.when(active)
        def _():
            for copy in halos(u):
                copy.wait_send()

        return carry

    lax.fori_loop(0, units, unit_body, 0)

    for role in roles:
        @pl.when(g == role)
        def _():
            run(role, orders[role]["end"])
            for make, args in started[role]:
                make(*args).wait_send()

    for i in range(2):
        pltpu.make_async_copy(
            H.at[g, pl.ds(i * half, half)], out_ref.at[0, pl.ds(i * half, half)], so.at[i]
        ).wait()


def shards(
    sections, domains,
    samples, w_source, w_self, w_message, w_output, norm_gain, tile_source, tile_count, tile_value,
):
    _, blocks, slots, blk, _ = tile_value.shape
    rows, width = samples.shape[1:]
    window = blocks + 2 * HB
    units = 2 * sections - 1
    chunks = MATS + blocks
    dma = pltpu.SemaphoreType.DMA
    anywhere = pl.BlockSpec(memory_space=pl.ANY)
    scalars = pl.BlockSpec(memory_space=pltpu.SMEM)
    flops = 2 * rows * width * (MATS * width + window * blk) * sections
    return pl.pallas_call(
        functools.partial(kernel, sections, domains),
        out_shape=jax.ShapeDtypeStruct((1, rows, width), jnp.bfloat16),
        in_specs=[scalars] * 2 + [anywhere] * 7,
        out_specs=anywhere,
        scratch_shapes=[
            pltpu.VMEM((sections, MATS, width, width), jnp.bfloat16),
            pltpu.VMEM((sections, rows, window * blk), jnp.bfloat16),
            pltpu.VMEM((sections, 1, width), jnp.float32),
            pltpu.VMEM((blocks, slots, blk, blk), jnp.bfloat16),
            pltpu.VMEM((sections, rows, width), jnp.bfloat16),
            pltpu.VMEM((units, window * blk, width), jnp.bfloat16),
            pltpu.VMEM((rows, width), jnp.float32),
            dma((MATS + 3,)),
            dma((sections, chunks)),
            dma((sections, MATS)),
            dma((sections, MATS, 2)),
            dma((sections,)),
            dma((2,)),
            dma((1,)),
            dma((units, 2)),
            dma((2, chunks)),
            dma((sections, chunks)),
            dma((sections, MATS)),
            dma((sections, MATS, 2)),
            dma((3,)),
            dma((sections, 2)),
            dma((1,)),
            dma((units, 2)),
            dma((2,)),
        ],
        compiler_params=pltpu.CompilerParams(
            collective_id=0, has_side_effects=True, vmem_limit_bytes=48 * 2**20
        ),
        cost_estimate=pl.CostEstimate(flops=flops, bytes_accessed=flops // 128, transcendentals=0),
    )(
        tile_source, tile_count, samples, w_source, w_self, w_message, w_output, norm_gain, tile_value
    )


def solution(mesh):
    return jax.shard_map(
        functools.partial(shards, mesh.shape["segment"], mesh.shape["dom"]),
        mesh=mesh,
        in_specs=(
            P(None, "dom", None),
            P("segment", None, None, None),
            P("segment", None, None, None),
            P("segment", None, None, None),
            P("segment", None, None, None),
            P("segment", None, None),
            P("segment", "dom", None),
            P("segment", "dom"),
            P("segment", "dom", None, None, None),
        ),
        out_specs=P("segment", "dom", None),
        check_vma=False,
    )
```

```python
import functools

import jax
import jax.numpy as jnp
from jax import lax
from jax.experimental import pallas as pl
from jax.experimental.pallas import tpu as pltpu
from jax.sharding import PartitionSpec as P

HB = 1
MESH = pl.DeviceIdType.MESH
MATS = 4

WEIGHT_TIMES = {
    (0, 1): (3.8, 6.5, 9.3, 12.0),
    (0, 2): (3.8, 6.5, 9.3, 12.0),
    (0, 3): (31.3, 34.0, 36.8, 39.5),
    (1, 2): (9.3, 14.8, 20.3, 23.0),
    (1, 3): (3.8, 6.5, 12.0, 17.5),
    (2, 1): (9.3, 14.8, 20.3, 23.0),
    (2, 3): (3.8, 6.5, 12.0, 17.5),
    (3, 1): (3.8, 6.5, 9.3, 12.0),
    (3, 2): (3.8, 6.5, 9.3, 12.0),
}
EDGE_TIMES = {
    (0, 1): (16.0, 20.0, 24.1, 28.3),
    (0, 2): (16.0, 20.0, 24.1, 28.3),
    (0, 3): (43.6, 32.3, 36.4, 40.5),
    (1, 2): (28.0, 32.0, 36.0, 40.0),
    (1, 3): (27.0, 31.2, 35.3, 39.5),
    (2, 1): (25.0, 29.0, 33.0, 37.0),
    (2, 3): (39.5, 27.0, 31.2, 35.3),
    (3, 1): (16.0, 25.7, 29.8, 34.0),
    (3, 2): (16.0, 25.7, 29.8, 34.0),
}
STATE_TIMES = {1: 24.0, 2: 20.0, 3: 21.6}
RELAY_TIME = 11.0
PIECES = 4
PIECE_TIMES = (0.9, 0.6, 1.2, 1.2)


def edge_target(role, section, block):
    if role == 0 and section in (1, 2):
        return 3 - section
    if role == 1 and section == 3 and block == 0:
        return 0
    if role == 2 and section == 3 and block > 0:
        return 0
    return None


def weight_target(role, section):
    if role == 3:
        return 3 - section
    if role == 1 and section == 3:
        return 0
    return None


def order_of(role, sections, blocks):
    events = []
    for s in range(1, sections):
        if s == role:
            continue
        for j, t in enumerate(WEIGHT_TIMES[role, s]):
            events.append((t, ("x", s, j)))
            events.append((t + 4.2, ("z", s, j)))
        for b in range(blocks):
            if edge_target(role, s, b) is not None:
                events.append((EDGE_TIMES[role, s][b], ("e", s, b)))
    if role in (1, 2):
        events.append((RELAY_TIME, ("r", 0, 0)))
    events.sort()
    times = {key: t for t, key in events}
    buckets = {}
    now = 1.0
    half = blocks // 2
    for u in range(2 * sections - 1):
        if u < sections and role != 0:
            continue
        s = max(u - sections + 1, 0)
        for p in range(PIECES):
            needs = []
            ready = now
            if s != role:
                mats = ((0,), (1,), (2, 3), ())[p]
                for j in mats:
                    needs += [("x", s, j), ("z", s, j)]
                    ready = max(ready, WEIGHT_TIMES[role, s][j] + 5.5)
                if p >= 2:
                    for b in range((p - 2) * half, (p - 1) * half):
                        ready = max(ready, EDGE_TIMES[role, s][b])
                        if ("e", s, b) in times:
                            needs.append(("e", s, b))
            if u == sections and p == 0 and role != 0:
                ready = max(ready, STATE_TIMES[role])
            chosen = [e for e in events if e[0] <= ready or e[1] in needs]
            if chosen:
                last = max(e[0] for e in chosen)
                chosen = [e for e in events if e[0] <= last]
                ready = max(ready, last)
            events = [e for e in events if e not in chosen]
            buckets[u, p] = [key for _, key in chosen]
            now = ready + PIECE_TIMES[p]
    buckets["end"] = [key for _, key in events]
    return buckets


def silu(v):
    half = 0.5 * v
    return half + half * jnp.tanh(half)


def kernel(
    sections, domains,
    source_ref, count_ref, samples_ref, wa_ref, wb_ref, wc_ref, wd_ref, gain_ref, tiles_ref,
    out_ref,
    W, E, G, T, H, PAD, BASE,
    l_sem, rx, rz, rc, rg, ra, rr, rh, sx, sf, sz, sc, sg, sa, sr, sh, so,
):
    g = lax.axis_index("segment")
    d = lax.axis_index("dom")
    w_refs = (wa_ref, wb_ref, wc_ref, wd_ref)
    _, blocks, slots, blk, _ = tiles_ref.shape
    window = blocks + 2 * HB
    rows = blocks * blk
    halo = HB * blk
    width = samples_ref.shape[-1]
    quarter = width // 4
    half = rows // 2
    per_half = blocks // 2
    units = 2 * sections - 1
    roles = range(sections)
    q = lax.rem(d, 4)
    zd = d + 2 - 4 * (q // 2)
    cd = d + 1 - 2 * lax.rem(d, 2)
    nxt, prv = lax.rem(d + 1, domains), lax.rem(d + domains - 1, domains)
    zq = lax.rem(zd, 4)
    cq = lax.rem(cd, 4)
    czq = lax.rem(q + 1 - 2 * lax.rem(q, 2) + 2, 4)

    def part(index):
        return pl.ds(pl.multiple_of(index * quarter, quarter), quarter)

    def remote(src, dst, send, recv, device):
        return pltpu.make_async_remote_copy(
            src_ref=src, dst_ref=dst, send_sem=send, recv_sem=recv,
            device_id=device, device_id_type=MESH,
        )

    def piece_of(s, j):
        if j < MATS:
            return W.at[s, j, part(q)]
        return E.at[s, pl.ds((j - MATS) * blk, blk)]

    def own(role, side, j):
        src = w_refs[j].at[0, 0, part(q)] if j < MATS else piece_of(role, j)
        to = role ^ (1 + side)
        return remote(src, piece_of(role, j), sx.at[side, j], rx.at[role, j], (to, d))

    def forward(s, j, to):
        return remote(piece_of(s, j), piece_of(s, j), sf.at[s, j], rx.at[s, j], (to, d))

    def to_pair(s, j):
        return remote(W.at[s, j, part(q)], W.at[s, j, part(q)], sz.at[s, j], rz.at[s, j], (g, zd))

    def to_core(s, j, kind):
        at = part(zq if kind else q)
        return remote(W.at[s, j, at], W.at[s, j, at], sc.at[s, j, kind], rc.at[s, j, kind], (g, cd))

    def wait_pair(s, j):
        remote(W.at[s, j, part(zq)], W.at[s, j, part(zq)], sz.at[s, j], rz.at[s, j], (g, zd)).wait_recv()

    def wait_core(s, j):
        for kind, index in enumerate((cq, czq)):
            at = part(index)
            remote(W.at[s, j, at], W.at[s, j, at], sc.at[s, j, kind], rc.at[s, j, kind], (g, cd)).wait_recv()

    def wait_block(s, b):
        at = pl.ds(b * blk, blk)
        remote(E.at[s, at], E.at[s, at], sf.at[s, MATS + b], rx.at[s, MATS + b], (g, cd)).wait_recv()

    def gain(role, k):
        to = role ^ (1 + k)
        return remote(gain_ref.at[pl.ds(0, 1)], G.at[pl.ds(role, 1)], sg.at[k], rg.at[role], (to, d))

    def wait_gain(s):
        remote(gain_ref.at[pl.ds(0, 1)], G.at[pl.ds(s, 1)], sg.at[0], rg.at[s], (g, cd)).wait_recv()

    def state(n, h):
        at = pl.ds(h * half, half)
        ref = H.at[n, at]
        last = sections - 1
        if n == last:
            return remote(ref, ref, sa.at[n, h], rr.at[0], (1 + h, d))
        return remote(ref, ref, sa.at[n, h], ra.at[h], (n, d))

    def relay(role):
        last = sections - 1
        ref = H.at[last, pl.ds((role - 1) * half, half)]
        return remote(ref, ref, sr.at[0], ra.at[role - 1], (last, d))

    def wait_state(n, h):
        ref = H.at[n, pl.ds(h * half, half)]
        remote(ref, ref, sr.at[0], ra.at[h], (g, cd)).wait_recv()

    def halos(u):
        first = PAD.at[u, pl.ds(halo, halo)]
        final = PAD.at[u, pl.ds(rows, halo)]
        return (
            remote(final, PAD.at[u, pl.ds(0, halo)], sh.at[u, 0], rh.at[u, 0], (g, nxt)),
            remote(first, PAD.at[u, pl.ds(halo + rows, halo)], sh.at[u, 1], rh.at[u, 1], (g, prv)),
        )

    def local_copies():
        made = [pltpu.make_async_copy(tiles_ref.at[0], T, l_sem.at[0])]
        made += [
            pltpu.make_async_copy(w_refs[j].at[0, 0], W.at[g, j], l_sem.at[1 + j]) for j in range(MATS)
        ]
        made.append(
            pltpu.make_async_copy(gain_ref.at[pl.ds(0, 1)], G.at[pl.ds(g, 1)], l_sem.at[1 + MATS])
        )
        return made

    samples_copy = pltpu.make_async_copy(samples_ref, H, l_sem.at[2 + MATS])

    for copy in local_copies():
        copy.start()

    @pl.when(g == 0)
    def _():
        samples_copy.start()

    barrier = pltpu.get_barrier_semaphore()
    peers = [(lax.rem(g + k, sections), d) for k in range(1, sections)]
    peers += [(g, zd), (g, cd), (g, nxt), (g, prv)]
    for peer in peers:
        pl.semaphore_signal(barrier, inc=1, device_id=peer, device_id_type=MESH)
    pl.semaphore_wait(barrier, len(peers))

    started = {role: [] for role in roles}

    def begin(role, make, *args):
        make(*args).start()
        started[role].append((make, args))

    for role in roles[1:]:
        @pl.when(g == role)
        def _():
            for j in range(MATS if role < 3 else 2):
                for side in range(2):
                    begin(role, own, role, side, j)
            for k in range(3):
                begin(role, gain, role, k)

    copies = local_copies()

    def send_senders(u, s, n):
        for i in range(2):
            at = pl.ds(i * half, half)
            v = jnp.dot(H[n, at], W[s, 0], preferred_element_type=jnp.float32)
            PAD[u, pl.ds(halo + i * half, half)] = silu(v).astype(jnp.bfloat16)
        for copy in halos(u):
            copy.start()

    def home_senders(u, carry):
        send_senders(u, 0, sections - 1 - u)
        return carry

    copies[1].wait()

    @pl.when(g == 0)
    def _():
        samples_copy.wait()
        lax.fori_loop(0, sections, home_senders, 0)

    copies[0].wait()
    total = blocks * domains
    base = d * blocks - HB

    def densify(b, carry):
        local = [lax.rem(source_ref[0, b, k] - base + total, total) for k in range(slots)]
        count = count_ref[0, b]
        at = pl.ds(pl.multiple_of(b * blk, blk), blk)
        for w in range(window):
            summed = jnp.zeros((blk, blk), jnp.float32)
            for k in range(slots):
                keep = ((local[k] == w) & (count > k)).astype(jnp.float32)
                summed += T[b, k].astype(jnp.float32) * keep
            E[g, at, w * blk : (w + 1) * blk] = summed.astype(jnp.bfloat16)
        return carry

    lax.fori_loop(0, blocks, densify, 0)

    for role in (1, 2):
        @pl.when(g == role)
        def _():
            for b in range(blocks):
                begin(role, own, role, role - 1, MATS + b)
                if b == 0:
                    begin(role, own, role, 2 - role, MATS)

    for copy in copies[2:]:
        copy.wait()

    def run(role, keys):
        for kind, s, j in keys:
            if kind == "x":
                forward(s, j, 0).wait_recv()
                begin(role, to_core, s, j, 0)
                begin(role, to_pair, s, j)
                to = weight_target(role, s)
                if to is not None:
                    begin(role, forward, s, j, to)
                if role == 3:
                    side = (to ^ role) - 1
                    if j < 2:
                        begin(role, own, role, side, j + 2)
                    if j == 3:
                        order = range(blocks)
                        if to == 2:
                            order = [*range(1, blocks), 0]
                        for b in order:
                            begin(role, own, role, side, MATS + b)
            elif kind == "z":
                wait_pair(s, j)
                begin(role, to_core, s, j, 1)
            elif kind == "e":
                wait_block(s, j)
                begin(role, forward, s, MATS + j, edge_target(role, s, j))
            else:
                ref = H.at[sections - 1, pl.ds((role - 1) * half, half)]
                remote(ref, ref, sr.at[0], rr.at[0], (g, cd)).wait_recv()
                begin(role, relay, role)
                for b in range(1, blocks):
                    begin(role, own, role, 2 - role, MATS + b)

    orders = {role: order_of(role, sections, blocks) for role in roles}

    def poll(u, p):
        for role in roles:
            for (unit, piece), keys in [kv for kv in orders[role].items() if kv[0] != "end"]:
                if piece == p and keys:
                    pl.when((g == role) & (u == unit))(functools.partial(run, role, keys))

    def unit_body(u, carry):
        s = jnp.maximum(u - (sections - 1), 0)
        n = jnp.where(u < sections, sections - 1 - u, g)
        active = (u >= sections) | (g == 0)
        fetched = s != g

        poll(u, 0)

        @pl.when(u >= sections)
        def _():
            @pl.when(fetched)
            def _():
                wait_core(s, 0)

            @pl.when((u == sections) & (g != 0))
            def _():
                for h in range(2):
                    wait_state(g, h)

            send_senders(u, s, n)

        poll(u, 1)

        @pl.when(active)
        def _():
            @pl.when(fetched)
            def _():
                wait_core(s, 1)

            for i in range(2):
                at = pl.ds(i * half, half)
                BASE[at] = jnp.dot(H[n, at], W[s, 1], preferred_element_type=jnp.float32)

        for i in range(2):
            poll(u, 2 + i)

            @pl.when(active)
            def _():
                @pl.when(fetched)
                def _():
                    if i == 0:
                        wait_core(s, 2)
                        wait_core(s, 3)
                        wait_gain(s)
                    for b in range(i * per_half, (i + 1) * per_half):
                        passed = jnp.bool_(False)
                        for role in roles:
                            for section in roles[1:]:
                                if section != role and edge_target(role, section, b) is not None:
                                    passed = passed | ((g == role) & (s == section))

                        @pl.when(jnp.logical_not(passed))
                        def _():
                            wait_block(s, b)

                if i == 0:
                    for copy in halos(u):
                        copy.wait_recv()
                at = pl.ds(i * half, half)
                gathered = jnp.dot(E[s, at], PAD[u], preferred_element_type=jnp.float32)
                mixed = BASE[at] + jnp.dot(
                    gathered.astype(jnp.bfloat16), W[s, 2], preferred_element_type=jnp.float32
                )
                scale = lax.rsqrt(jnp.mean(mixed * mixed, axis=-1, keepdims=True) + 1e-05)
                update = silu(mixed * scale * G[s]).astype(jnp.bfloat16)
                result = H[n, at].astype(jnp.float32) + jnp.dot(
                    update, W[s, 3], preferred_element_type=jnp.float32
                )
                H[n, at] = result.astype(jnp.bfloat16)

            for unit in range(sections - 1):
                @pl.when((g == 0) & (u == unit))
                def _():
                    begin(0, state, sections - 1 - unit, i)

            @pl.when(u == units - 1)
            def _():
                pltpu.make_async_copy(
                    H.at[g, pl.ds(i * half, half)], out_ref.at[0, pl.ds(i * half, half)], so.at[i]
                ).start()

        @pl.when(active)
        def _():
            for copy in halos(u):
                copy.wait_send()

        return carry

    lax.fori_loop(0, units, unit_body, 0)

    for role in roles:
        @pl.when(g == role)
        def _():
            run(role, orders[role]["end"])
            for make, args in started[role]:
                make(*args).wait_send()

    for i in range(2):
        pltpu.make_async_copy(
            H.at[g, pl.ds(i * half, half)], out_ref.at[0, pl.ds(i * half, half)], so.at[i]
        ).wait()


def shards(
    sections, domains,
    samples, w_source, w_self, w_message, w_output, norm_gain, tile_source, tile_count, tile_value,
):
    _, blocks, slots, blk, _ = tile_value.shape
    rows, width = samples.shape[1:]
    window = blocks + 2 * HB
    units = 2 * sections - 1
    chunks = MATS + blocks
    dma = pltpu.SemaphoreType.DMA
    anywhere = pl.BlockSpec(memory_space=pl.ANY)
    scalars = pl.BlockSpec(memory_space=pltpu.SMEM)
    flops = 2 * rows * width * (MATS * width + window * blk) * sections
    return pl.pallas_call(
        functools.partial(kernel, sections, domains),
        out_shape=jax.ShapeDtypeStruct((1, rows, width), jnp.bfloat16),
        in_specs=[scalars] * 2 + [anywhere] * 7,
        out_specs=anywhere,
        scratch_shapes=[
            pltpu.VMEM((sections, MATS, width, width), jnp.bfloat16),
            pltpu.VMEM((sections, rows, window * blk), jnp.bfloat16),
            pltpu.VMEM((sections, 1, width), jnp.float32),
            pltpu.VMEM((blocks, slots, blk, blk), jnp.bfloat16),
            pltpu.VMEM((sections, rows, width), jnp.bfloat16),
            pltpu.VMEM((units, window * blk, width), jnp.bfloat16),
            pltpu.VMEM((rows, width), jnp.float32),
            dma((MATS + 3,)),
            dma((sections, chunks)),
            dma((sections, MATS)),
            dma((sections, MATS, 2)),
            dma((sections,)),
            dma((2,)),
            dma((1,)),
            dma((units, 2)),
            dma((2, chunks)),
            dma((sections, chunks)),
            dma((sections, MATS)),
            dma((sections, MATS, 2)),
            dma((3,)),
            dma((sections, 2)),
            dma((1,)),
            dma((units, 2)),
            dma((2,)),
        ],
        compiler_params=pltpu.CompilerParams(
            collective_id=0, has_side_effects=True, vmem_limit_bytes=60 * 2**20
        ),
        cost_estimate=pl.CostEstimate(flops=flops, bytes_accessed=flops // 128, transcendentals=0),
    )(
        tile_source, tile_count, samples, w_source, w_self, w_message, w_output, norm_gain, tile_value
    )


def solution(mesh):
    return jax.shard_map(
        functools.partial(shards, mesh.shape["segment"], mesh.shape["dom"]),
        mesh=mesh,
        in_specs=(
            P(None, "dom", None),
            P("segment", None, None, None),
            P("segment", None, None, None),
            P("segment", None, None, None),
            P("segment", None, None, None),
            P("segment", None, None),
            P("segment", "dom", None),
            P("segment", "dom"),
            P("segment", "dom", None, None, None),
        ),
        out_specs=P("segment", "dom", None),
        check_vma=False,
    )
```

```python
import functools

import jax
import jax.numpy as jnp
from jax import lax
from jax.experimental import pallas as pl
from jax.experimental.pallas import tpu as pltpu
from jax.sharding import PartitionSpec as P

HB = 1
MESH = pl.DeviceIdType.MESH
MATS = 4

EDGES_BY_LAST = {1: [0], 2: [0]}
WEIGHTS_BY_FIRST = {1: [0], 2: []}
WHOLE_WEIGHTS = {1: [], 2: [0, 3]}
BLOCKS_BY_ONE = 1
BLOCK_ORDER = {2: [3, 2, 0, 1], 1: [0, 3, 2, 1]}
RELAYS = (2, 1)
RELAY_FIRST = True
ORDER = {
    0: {
        (0, 2): [('x', 1, 0)],
        (2, 3): [('x', 1, 3)],
        (3, 1): [('x', 2, 3)],
        (4, 0): [('x', 1, 1), ('x', 2, 0), ('x', 2, 2), ('z', 1, 1), ('e', 1, 1), ('x', 2, 1), ('e', 1, 2), ('e', 2, 1), ('z', 2, 2), ('x', 1, 2), ('z', 1, 3), ('z', 1, 0), ('z', 2, 1)],
        (4, 2): [('e', 1, 3), ('e', 2, 2), ('x', 3, 1), ('z', 1, 2), ('z', 2, 0), ('e', 2, 3), ('x', 3, 0)],
        (5, 0): [('z', 2, 3)],
        (5, 2): [('z', 3, 1), ('x', 3, 2), ('x', 3, 3), ('z', 3, 0)],
        (6, 0): [('z', 3, 2)],
        (6, 2): [('z', 3, 3)],
        (-1, 0): [],
    },
    1: {
        (4, 0): [('x', 3, 1), ('x', 3, 0), ('z', 3, 1), ('x', 2, 0), ('x', 3, 2), ('x', 2, 1), ('z', 3, 0), ('r', 3, 1), ('x', 3, 3), ('x', 2, 2), ('z', 2, 1), ('z', 2, 0)],
        (4, 2): [('z', 3, 3), ('x', 2, 3)],
        (5, 2): [('z', 3, 2), ('z', 2, 2), ('e', 3, 0), ('z', 2, 3)],
        (-1, 0): [],
    },
    2: {
        (4, 0): [('x', 3, 0), ('x', 1, 0), ('x', 1, 1), ('z', 3, 0), ('x', 3, 3), ('x', 3, 1), ('x', 1, 2), ('r', 3, 0), ('z', 3, 3), ('z', 3, 1), ('z', 1, 2), ('x', 3, 2), ('z', 1, 1), ('z', 1, 0)],
        (4, 2): [('z', 3, 2), ('x', 1, 3), ('e', 3, 2), ('z', 1, 3)],
        (5, 2): [('e', 3, 1), ('e', 3, 3)],
        (-1, 0): [],
    },
    3: {
        (4, 0): [('x', 2, 0), ('x', 1, 1), ('x', 2, 1), ('x', 2, 2), ('x', 1, 0), ('z', 2, 0), ('x', 1, 2), ('e', 2, 0), ('z', 1, 1), ('e', 1, 0), ('x', 1, 3), ('z', 2, 1), ('x', 2, 3), ('z', 1, 2), ('z', 1, 0), ('z', 2, 2)],
        (4, 2): [('z', 1, 3)],
        (5, 2): [('z', 2, 3)],
        (-1, 0): [],
    },
}


def edge_target(role, section, block):
    if section in EDGES_BY_LAST and role in (0, 3):
        if (block in EDGES_BY_LAST[section]) == (role == 3):
            return 3 - section
    if section == 3 and role == (1 if block < BLOCKS_BY_ONE else 2):
        return 0
    return None


def weight_target(role, section, j):
    if section in WEIGHTS_BY_FIRST and role in (0, 3):
        if (j in WEIGHTS_BY_FIRST[section]) == (role == 0):
            return 3 - section
    if role == 1 and section == 3:
        return 0
    return None


def silu(v):
    half = 0.5 * v
    return half + half * jnp.tanh(half)


def kernel(
    sections, domains,
    source_ref, count_ref, samples_ref, wa_ref, wb_ref, wc_ref, wd_ref, gain_ref, tiles_ref,
    out_ref,
    W, E, G, T, H, PAD, BASE,
    l_sem, rx, rz, rc, rg, ra, rr, rh, sx, sf, sz, sc, sg, sa, sr, sh, so,
):
    g = lax.axis_index("segment")
    d = lax.axis_index("dom")
    w_refs = (wa_ref, wb_ref, wc_ref, wd_ref)
    _, blocks, slots, blk, _ = tiles_ref.shape
    window = blocks + 2 * HB
    rows = blocks * blk
    halo = HB * blk
    width = samples_ref.shape[-1]
    quarter = width // 4
    half = rows // 2
    per_half = blocks // 2
    units = 2 * sections - 1
    roles = range(sections)
    q = lax.rem(d, 4)
    zd = d + 2 - 4 * (q // 2)
    cd = d + 1 - 2 * lax.rem(d, 2)
    nxt, prv = lax.rem(d + 1, domains), lax.rem(d + domains - 1, domains)
    zq = lax.rem(zd, 4)
    cq = lax.rem(cd, 4)
    czq = lax.rem(q + 1 - 2 * lax.rem(q, 2) + 2, 4)

    def part(index):
        return pl.ds(pl.multiple_of(index * quarter, quarter), quarter)

    def remote(src, dst, send, recv, device):
        return pltpu.make_async_remote_copy(
            src_ref=src, dst_ref=dst, send_sem=send, recv_sem=recv,
            device_id=device, device_id_type=MESH,
        )

    def piece_of(s, j):
        if j < MATS:
            return W.at[s, j, part(q)]
        return E.at[s, pl.ds((j - MATS) * blk, blk)]

    def own(role, side, j):
        src = w_refs[j].at[0, 0, part(q)] if j < MATS else piece_of(role, j)
        to = role ^ (1 + side)
        return remote(src, piece_of(role, j), sx.at[side, j], rx.at[role, j], (to, d))

    def forward(s, j, to):
        return remote(piece_of(s, j), piece_of(s, j), sf.at[s, j], rx.at[s, j], (to, d))

    def to_pair(s, j):
        return remote(W.at[s, j, part(q)], W.at[s, j, part(q)], sz.at[s, j], rz.at[s, j], (g, zd))

    def to_core(s, j, kind):
        at = part(zq if kind else q)
        return remote(W.at[s, j, at], W.at[s, j, at], sc.at[s, j, kind], rc.at[s, j, kind], (g, cd))

    def wait_pair(s, j):
        remote(W.at[s, j, part(zq)], W.at[s, j, part(zq)], sz.at[s, j], rz.at[s, j], (g, zd)).wait_recv()

    def wait_core(s, j):
        for kind, index in enumerate((cq, czq)):
            at = part(index)
            remote(W.at[s, j, at], W.at[s, j, at], sc.at[s, j, kind], rc.at[s, j, kind], (g, cd)).wait_recv()

    def wait_block(s, b):
        at = pl.ds(b * blk, blk)
        remote(E.at[s, at], E.at[s, at], sf.at[s, MATS + b], rx.at[s, MATS + b], (g, cd)).wait_recv()

    def gain(role, k):
        to = role ^ (1 + k)
        return remote(gain_ref.at[pl.ds(0, 1)], G.at[pl.ds(role, 1)], sg.at[k], rg.at[role], (to, d))

    def wait_gain(s):
        remote(gain_ref.at[pl.ds(0, 1)], G.at[pl.ds(s, 1)], sg.at[0], rg.at[s], (g, cd)).wait_recv()

    def state(n, h):
        at = pl.ds(h * half, half)
        ref = H.at[n, at]
        last = sections - 1
        if n == last:
            return remote(ref, ref, sa.at[n, h], rr.at[h], (RELAYS[h], d))
        return remote(ref, ref, sa.at[n, h], ra.at[h], (n, d))

    def relay(h):
        last = sections - 1
        ref = H.at[last, pl.ds(h * half, half)]
        return remote(ref, ref, sr.at[h], ra.at[h], (last, d))

    def whole(role, j):
        at = part(zq)
        src = w_refs[j].at[0, 0, at]
        return remote(src, W.at[role, j, at], sz.at[role, j], rz.at[role, j], (0, d))

    def wait_state(n, h):
        ref = H.at[n, pl.ds(h * half, half)]
        remote(ref, ref, sr.at[0], ra.at[h], (g, cd)).wait_recv()

    def halos(u):
        first = PAD.at[u, pl.ds(halo, halo)]
        final = PAD.at[u, pl.ds(rows, halo)]
        return (
            remote(final, PAD.at[u, pl.ds(0, halo)], sh.at[u, 0], rh.at[u, 0], (g, nxt)),
            remote(first, PAD.at[u, pl.ds(halo + rows, halo)], sh.at[u, 1], rh.at[u, 1], (g, prv)),
        )

    def local_copies():
        made = [pltpu.make_async_copy(tiles_ref.at[0], T, l_sem.at[0])]
        made += [
            pltpu.make_async_copy(w_refs[j].at[0, 0], W.at[g, j], l_sem.at[1 + j]) for j in range(MATS)
        ]
        made.append(
            pltpu.make_async_copy(gain_ref.at[pl.ds(0, 1)], G.at[pl.ds(g, 1)], l_sem.at[1 + MATS])
        )
        return made

    samples_copy = pltpu.make_async_copy(samples_ref, H, l_sem.at[2 + MATS])

    for copy in local_copies():
        copy.start()

    @pl.when(g == 0)
    def _():
        samples_copy.start()

    barrier = pltpu.get_barrier_semaphore()
    peers = [(lax.rem(g + k, sections), d) for k in range(1, sections)]
    peers += [(g, zd), (g, cd), (g, nxt), (g, prv)]
    for peer in peers:
        pl.semaphore_signal(barrier, inc=1, device_id=peer, device_id_type=MESH)
    pl.semaphore_wait(barrier, len(peers))

    started = {role: [] for role in roles}

    def begin(role, make, *args):
        make(*args).start()
        started[role].append((make, args))

    for role in roles[1:]:
        @pl.when(g == role)
        def _():
            for j in range(MATS if role < 3 else 2):
                for side in range(2):
                    begin(role, own, role, side, j)
            for k in range(3):
                begin(role, gain, role, k)

    copies = local_copies()

    def send_senders(u, s, n):
        for i in range(2):
            at = pl.ds(i * half, half)
            v = jnp.dot(H[n, at], W[s, 0], preferred_element_type=jnp.float32)
            PAD[u, pl.ds(halo + i * half, half)] = silu(v).astype(jnp.bfloat16)
        for copy in halos(u):
            copy.start()

    def home_senders(u, carry):
        send_senders(u, 0, sections - 1 - u)
        return carry

    copies[1].wait()

    @pl.when(g == 0)
    def _():
        samples_copy.wait()
        lax.fori_loop(0, sections, home_senders, 0)

    copies[0].wait()
    total = blocks * domains
    base = d * blocks - HB

    def densify(b, carry):
        local = [lax.rem(source_ref[0, b, k] - base + total, total) for k in range(slots)]
        count = count_ref[0, b]
        at = pl.ds(pl.multiple_of(b * blk, blk), blk)
        for w in range(window):
            summed = jnp.zeros((blk, blk), jnp.float32)
            for k in range(slots):
                keep = ((local[k] == w) & (count > k)).astype(jnp.float32)
                summed += T[b, k].astype(jnp.float32) * keep
            E[g, at, w * blk : (w + 1) * blk] = summed.astype(jnp.bfloat16)
        return carry

    lax.fori_loop(0, blocks, densify, 0)

    for role in (1, 2):
        @pl.when(g == role)
        def _():
            for j in WHOLE_WEIGHTS[role]:
                begin(role, whole, role, j)
            for b in range(blocks):
                begin(role, own, role, role - 1, MATS + b)
                if b == 0:
                    begin(role, own, role, 2 - role, MATS)
            if not (RELAY_FIRST and role in RELAYS):
                for b in range(1, blocks):
                    begin(role, own, role, 2 - role, MATS + b)

    for copy in copies[2:]:
        copy.wait()

    def run(role, keys):
        for kind, s, j in keys:
            if kind == "x":
                forward(s, j, 0).wait_recv()
                begin(role, to_core, s, j, 0)
                if role != 0 or j not in WHOLE_WEIGHTS.get(s, ()):
                    begin(role, to_pair, s, j)
                to = weight_target(role, s, j)
                if to is not None:
                    begin(role, forward, s, j, to)
                if role == 3:
                    other = 3 - s
                    side = (other ^ role) - 1
                    if j < 2:
                        begin(role, own, role, side, j + 2)
                    if j == 3:
                        for b in BLOCK_ORDER[other]:
                            begin(role, own, role, side, MATS + b)
            elif kind == "z":
                wait_pair(s, j)
                begin(role, to_core, s, j, 1)
            elif kind == "e":
                wait_block(s, j)
                begin(role, forward, s, MATS + j, edge_target(role, s, j))
            else:
                ref = H.at[sections - 1, pl.ds(j * half, half)]
                remote(ref, ref, sr.at[j], rr.at[j], (g, cd)).wait_recv()
                begin(role, relay, j)
                if RELAY_FIRST and j == max(h for h in range(2) if RELAYS[h] == role):
                    for b in range(1, blocks):
                        begin(role, own, role, 2 - role, MATS + b)

    def poll(u, p):
        for role in roles:
            for (unit, piece), keys in ORDER[role].items():
                if piece == p and keys:
                    pl.when((g == role) & (u == unit))(functools.partial(run, role, keys))

    def unit_body(u, carry):
        s = jnp.maximum(u - (sections - 1), 0)
        n = jnp.where(u < sections, sections - 1 - u, g)
        active = (u >= sections) | (g == 0)
        fetched = s != g

        poll(u, 0)

        @pl.when(u >= sections)
        def _():
            @pl.when(fetched)
            def _():
                wait_core(s, 0)

            @pl.when((u == sections) & (g != 0))
            def _():
                for h in range(2):
                    wait_state(g, h)

            send_senders(u, s, n)

        poll(u, 1)

        @pl.when(active)
        def _():
            @pl.when(fetched)
            def _():
                wait_core(s, 1)

            for i in range(2):
                at = pl.ds(i * half, half)
                BASE[at] = jnp.dot(H[n, at], W[s, 1], preferred_element_type=jnp.float32)

        for i in range(2):
            poll(u, 2 + i)

            @pl.when(active)
            def _():
                @pl.when(fetched)
                def _():
                    if i == 0:
                        wait_core(s, 2)
                        wait_core(s, 3)
                        wait_gain(s)
                    for b in range(i * per_half, (i + 1) * per_half):
                        passed = jnp.bool_(False)
                        for role in roles:
                            for section in roles[1:]:
                                if section != role and edge_target(role, section, b) is not None:
                                    passed = passed | ((g == role) & (s == section))

                        @pl.when(jnp.logical_not(passed))
                        def _():
                            wait_block(s, b)

                if i == 0:
                    for copy in halos(u):
                        copy.wait_recv()
                at = pl.ds(i * half, half)
                gathered = jnp.dot(E[s, at], PAD[u], preferred_element_type=jnp.float32)
                mixed = BASE[at] + jnp.dot(
                    gathered.astype(jnp.bfloat16), W[s, 2], preferred_element_type=jnp.float32
                )
                scale = lax.rsqrt(jnp.mean(mixed * mixed, axis=-1, keepdims=True) + 1e-05)
                update = silu(mixed * scale * G[s]).astype(jnp.bfloat16)
                result = H[n, at].astype(jnp.float32) + jnp.dot(
                    update, W[s, 3], preferred_element_type=jnp.float32
                )
                H[n, at] = result.astype(jnp.bfloat16)

            for unit in range(sections - 1):
                @pl.when((g == 0) & (u == unit))
                def _():
                    begin(0, state, sections - 1 - unit, i)

            @pl.when(u == units - 1)
            def _():
                pltpu.make_async_copy(
                    H.at[g, pl.ds(i * half, half)], out_ref.at[0, pl.ds(i * half, half)], so.at[i]
                ).start()

        @pl.when(active)
        def _():
            for copy in halos(u):
                copy.wait_send()

        return carry

    lax.fori_loop(0, units, unit_body, 0)

    for role in roles:
        @pl.when(g == role)
        def _():
            run(role, ORDER[role][-1, 0])
            for make, args in started[role]:
                make(*args).wait_send()

    for i in range(2):
        pltpu.make_async_copy(
            H.at[g, pl.ds(i * half, half)], out_ref.at[0, pl.ds(i * half, half)], so.at[i]
        ).wait()


def shards(
    sections, domains,
    samples, w_source, w_self, w_message, w_output, norm_gain, tile_source, tile_count, tile_value,
):
    _, blocks, slots, blk, _ = tile_value.shape
    rows, width = samples.shape[1:]
    window = blocks + 2 * HB
    units = 2 * sections - 1
    chunks = MATS + blocks
    dma = pltpu.SemaphoreType.DMA
    anywhere = pl.BlockSpec(memory_space=pl.ANY)
    scalars = pl.BlockSpec(memory_space=pltpu.SMEM)
    flops = 2 * rows * width * (MATS * width + window * blk) * sections
    return pl.pallas_call(
        functools.partial(kernel, sections, domains),
        out_shape=jax.ShapeDtypeStruct((1, rows, width), jnp.bfloat16),
        in_specs=[scalars] * 2 + [anywhere] * 7,
        out_specs=anywhere,
        scratch_shapes=[
            pltpu.VMEM((sections, MATS, width, width), jnp.bfloat16),
            pltpu.VMEM((sections, rows, window * blk), jnp.bfloat16),
            pltpu.VMEM((sections, 1, width), jnp.float32),
            pltpu.VMEM((blocks, slots, blk, blk), jnp.bfloat16),
            pltpu.VMEM((sections, rows, width), jnp.bfloat16),
            pltpu.VMEM((units, window * blk, width), jnp.bfloat16),
            pltpu.VMEM((rows, width), jnp.float32),
            dma((MATS + 3,)),
            dma((sections, chunks)),
            dma((sections, MATS)),
            dma((sections, MATS, 2)),
            dma((sections,)),
            dma((2,)),
            dma((2,)),
            dma((units, 2)),
            dma((2, chunks)),
            dma((sections, chunks)),
            dma((sections, MATS)),
            dma((sections, MATS, 2)),
            dma((3,)),
            dma((sections, 2)),
            dma((2,)),
            dma((units, 2)),
            dma((2,)),
        ],
        compiler_params=pltpu.CompilerParams(
            collective_id=0, has_side_effects=True, vmem_limit_bytes=60 * 2**20
        ),
        cost_estimate=pl.CostEstimate(flops=flops, bytes_accessed=flops // 128, transcendentals=0),
    )(
        tile_source, tile_count, samples, w_source, w_self, w_message, w_output, norm_gain, tile_value
    )


def solution(mesh):
    return jax.shard_map(
        functools.partial(shards, mesh.shape["segment"], mesh.shape["dom"]),
        mesh=mesh,
        in_specs=(
            P(None, "dom", None),
            P("segment", None, None, None),
            P("segment", None, None, None),
            P("segment", None, None, None),
            P("segment", None, None, None),
            P("segment", None, None),
            P("segment", "dom", None),
            P("segment", "dom"),
            P("segment", "dom", None, None, None),
        ),
        out_specs=P("segment", "dom", None),
        check_vma=False,
    )
```

```python
import functools

import jax
import jax.numpy as jnp
from jax import lax
from jax.experimental import pallas as pl
from jax.experimental.pallas import tpu as pltpu
from jax.sharding import PartitionSpec as P

HB = 1
MESH = pl.DeviceIdType.MESH
MATS = 4

EDGES_BY_LAST = {1: [0, 1], 2: [3]}
WEIGHTS_BY_FIRST = {1: [0, 3], 2: [1, 2]}
WHOLE_WEIGHTS = {1: [], 2: [0, 2, 3]}
BLOCKS_BY_ONE = 1
BLOCK_ORDER = {2: [2, 1, 3, 0], 1: [0, 1, 2, 3]}
RELAYS = (2, 1)
RELAY_FIRST = True
ORDER = {
    0: {
        (0, 2): [('x', 1, 0), ('x', 1, 1), ('x', 2, 1)],
        (2, 1): [('x', 2, 0)],
        (3, 1): [('z', 2, 0), ('x', 2, 3)],
        (4, 0): [('x', 2, 2), ('z', 1, 0), ('z', 2, 3)],
        (4, 1): [('e', 2, 0), ('z', 1, 1), ('z', 2, 1), ('x', 1, 3)],
        (4, 2): [('x', 1, 2), ('z', 1, 3), ('e', 1, 3), ('z', 2, 2), ('x', 3, 1), ('e', 1, 2), ('z', 1, 2), ('e', 2, 1), ('e', 2, 2), ('x', 3, 0)],
        (5, 2): [('x', 3, 3), ('x', 3, 2)],
        (6, 0): [('z', 3, 0), ('z', 3, 1)],
        (6, 2): [('z', 3, 2), ('z', 3, 3)],
        (-1, 0): [],
    },
    1: {
        (4, 0): [('x', 3, 1), ('x', 2, 1), ('x', 3, 0), ('x', 2, 0), ('z', 3, 1), ('r', 3, 1), ('x', 3, 3), ('x', 3, 2), ('z', 2, 0), ('z', 3, 0)],
        (4, 1): [('x', 2, 3), ('z', 3, 3)],
        (4, 2): [('z', 2, 1), ('z', 3, 2)],
        (5, 0): [('z', 2, 3)],
        (5, 2): [('x', 2, 2), ('z', 2, 2)],
        (6, 1): [('e', 3, 0)],
        (-1, 0): [],
    },
    2: {
        (4, 0): [('x', 3, 0), ('x', 3, 1), ('z', 3, 1), ('x', 3, 2), ('x', 1, 1), ('x', 3, 3), ('x', 1, 0), ('r', 3, 0), ('z', 3, 2), ('x', 1, 2), ('z', 1, 0), ('z', 3, 0)],
        (4, 1): [('e', 3, 2), ('z', 1, 1)],
        (4, 2): [('z', 3, 3), ('z', 1, 2), ('e', 3, 1), ('x', 1, 3), ('e', 3, 3), ('z', 1, 3)],
        (-1, 0): [],
    },
    3: {
        (4, 0): [('x', 1, 0), ('x', 1, 1), ('x', 2, 1), ('x', 2, 0), ('x', 1, 2), ('x', 2, 2), ('z', 2, 1), ('z', 1, 1), ('x', 2, 3), ('z', 1, 0), ('e', 1, 0), ('z', 1, 2), ('x', 1, 3), ('z', 2, 0)],
        (4, 2): [('z', 2, 2), ('z', 1, 3), ('e', 1, 1), ('e', 2, 3), ('z', 2, 3)],
        (-1, 0): [],
    },
}


def edge_target(role, section, block):
    if section in EDGES_BY_LAST and role in (0, 3):
        if (block in EDGES_BY_LAST[section]) == (role == 3):
            return 3 - section
    if section == 3 and role == (1 if block < BLOCKS_BY_ONE else 2):
        return 0
    return None


def weight_target(role, section, j):
    if section in WEIGHTS_BY_FIRST and role in (0, 3):
        if (j in WEIGHTS_BY_FIRST[section]) == (role == 0):
            return 3 - section
    if role == 1 and section == 3:
        return 0
    return None


def silu(v):
    half = 0.5 * v
    return half + half * jnp.tanh(half)


def kernel(
    sections, domains,
    source_ref, count_ref, samples_ref, wa_ref, wb_ref, wc_ref, wd_ref, gain_ref, tiles_ref,
    out_ref,
    W, E, G, T, H, PAD, BASE,
    l_sem, rx, rz, rc, rg, ra, rr, rh, sx, sf, sz, sc, sg, sa, sr, sh, so,
):
    g = lax.axis_index("segment")
    d = lax.axis_index("dom")
    w_refs = (wa_ref, wb_ref, wc_ref, wd_ref)
    _, blocks, slots, blk, _ = tiles_ref.shape
    window = blocks + 2 * HB
    rows = blocks * blk
    halo = HB * blk
    width = samples_ref.shape[-1]
    quarter = width // 4
    half = rows // 2
    per_half = blocks // 2
    units = 2 * sections - 1
    roles = range(sections)
    q = lax.rem(d, 4)
    zd = d + 2 - 4 * (q // 2)
    cd = d + 1 - 2 * lax.rem(d, 2)
    nxt, prv = lax.rem(d + 1, domains), lax.rem(d + domains - 1, domains)
    zq = lax.rem(zd, 4)
    cq = lax.rem(cd, 4)
    czq = lax.rem(q + 1 - 2 * lax.rem(q, 2) + 2, 4)

    def part(index):
        return pl.ds(pl.multiple_of(index * quarter, quarter), quarter)

    def remote(src, dst, send, recv, device):
        return pltpu.make_async_remote_copy(
            src_ref=src, dst_ref=dst, send_sem=send, recv_sem=recv,
            device_id=device, device_id_type=MESH,
        )

    def piece_of(s, j):
        if j < MATS:
            return W.at[s, j, part(q)]
        return E.at[s, pl.ds((j - MATS) * blk, blk)]

    def own(role, side, j):
        src = w_refs[j].at[0, 0, part(q)] if j < MATS else piece_of(role, j)
        to = role ^ (1 + side)
        return remote(src, piece_of(role, j), sx.at[side, j], rx.at[role, j], (to, d))

    def forward(s, j, to):
        return remote(piece_of(s, j), piece_of(s, j), sf.at[s, j], rx.at[s, j], (to, d))

    def to_pair(s, j):
        return remote(W.at[s, j, part(q)], W.at[s, j, part(q)], sz.at[s, j], rz.at[s, j], (g, zd))

    def to_core(s, j, kind):
        at = part(zq if kind else q)
        return remote(W.at[s, j, at], W.at[s, j, at], sc.at[s, j, kind], rc.at[s, j, kind], (g, cd))

    def wait_pair(s, j):
        remote(W.at[s, j, part(zq)], W.at[s, j, part(zq)], sz.at[s, j], rz.at[s, j], (g, zd)).wait_recv()

    def wait_core(s, j):
        for kind, index in enumerate((cq, czq)):
            at = part(index)
            remote(W.at[s, j, at], W.at[s, j, at], sc.at[s, j, kind], rc.at[s, j, kind], (g, cd)).wait_recv()

    def wait_block(s, b):
        at = pl.ds(b * blk, blk)
        remote(E.at[s, at], E.at[s, at], sf.at[s, MATS + b], rx.at[s, MATS + b], (g, cd)).wait_recv()

    def gain(role, k):
        to = role ^ (1 + k)
        return remote(gain_ref.at[pl.ds(0, 1)], G.at[pl.ds(role, 1)], sg.at[k], rg.at[role], (to, d))

    def wait_gain(s):
        remote(gain_ref.at[pl.ds(0, 1)], G.at[pl.ds(s, 1)], sg.at[0], rg.at[s], (g, cd)).wait_recv()

    def state_part(n, k):
        at = (pl.ds(0, halo), pl.ds(rows - halo, halo), pl.ds(halo, rows - 2 * halo))[k]
        return H.at[n, at]

    def state(n, k):
        last = sections - 1
        ref = state_part(n, k)
        if n == last:
            return remote(ref, ref, sa.at[n, k], rr.at[k], (RELAYS[k // 2], d))
        return remote(ref, ref, sa.at[n, k], ra.at[k], (n, d))

    def relay(k):
        last = sections - 1
        ref = state_part(last, k)
        return remote(ref, ref, sr.at[k], ra.at[k], (last, d))

    def wait_state(n, k):
        ref = state_part(n, k)
        remote(ref, ref, sr.at[k], ra.at[k], (g, cd)).wait_recv()

    def whole(role, j):
        at = part(zq)
        src = w_refs[j].at[0, 0, at]
        return remote(src, W.at[role, j, at], sz.at[role, j], rz.at[role, j], (0, d))

    def halos(u):
        first = PAD.at[u, pl.ds(halo, halo)]
        final = PAD.at[u, pl.ds(rows, halo)]
        return (
            remote(final, PAD.at[u, pl.ds(0, halo)], sh.at[u, 0], rh.at[u, 0], (g, nxt)),
            remote(first, PAD.at[u, pl.ds(halo + rows, halo)], sh.at[u, 1], rh.at[u, 1], (g, prv)),
        )

    def local_copies():
        made = [pltpu.make_async_copy(tiles_ref.at[0], T, l_sem.at[0])]
        made += [
            pltpu.make_async_copy(w_refs[j].at[0, 0], W.at[g, j], l_sem.at[1 + j]) for j in range(MATS)
        ]
        made.append(
            pltpu.make_async_copy(gain_ref.at[pl.ds(0, 1)], G.at[pl.ds(g, 1)], l_sem.at[1 + MATS])
        )
        return made

    samples_copy = pltpu.make_async_copy(samples_ref, H, l_sem.at[2 + MATS])

    for copy in local_copies():
        copy.start()

    @pl.when(g == 0)
    def _():
        samples_copy.start()

    barrier = pltpu.get_barrier_semaphore()
    peers = [(lax.rem(g + k, sections), d) for k in range(1, sections)]
    peers += [(g, zd), (g, cd), (g, nxt), (g, prv)]
    for peer in peers:
        pl.semaphore_signal(barrier, inc=1, device_id=peer, device_id_type=MESH)
    pl.semaphore_wait(barrier, len(peers))

    started = {role: [] for role in roles}

    def begin(role, make, *args):
        make(*args).start()
        started[role].append((make, args))

    for role in roles[1:]:
        @pl.when(g == role)
        def _():
            for j in range(MATS if role < 3 else 2):
                for side in range(2):
                    begin(role, own, role, side, j)
            for k in range(3):
                begin(role, gain, role, k)

    copies = local_copies()

    def outer(ref, *index):
        return jnp.concatenate([ref[*index, :halo], ref[*index, rows - halo : rows]])

    def outer_senders(u, s, n):
        v = jnp.dot(outer(H, n), W[s, 0], preferred_element_type=jnp.float32)
        v = silu(v).astype(jnp.bfloat16)
        PAD[u, halo : 2 * halo] = v[:halo]
        PAD[u, rows : rows + halo] = v[halo:]
        for copy in halos(u):
            copy.start()

    def inner_senders(u, s, n):
        v = jnp.dot(H[n, halo : rows - halo], W[s, 0], preferred_element_type=jnp.float32)
        PAD[u, 2 * halo : rows] = silu(v).astype(jnp.bfloat16)

    def home_senders(u, carry):
        outer_senders(u, 0, sections - 1 - u)
        inner_senders(u, 0, sections - 1 - u)
        return carry

    copies[1].wait()

    @pl.when(g == 0)
    def _():
        samples_copy.wait()
        lax.fori_loop(0, sections, home_senders, 0)

    copies[0].wait()
    total = blocks * domains
    base = d * blocks - HB

    def densify(b, carry):
        local = [lax.rem(source_ref[0, b, k] - base + total, total) for k in range(slots)]
        count = count_ref[0, b]
        at = pl.ds(pl.multiple_of(b * blk, blk), blk)
        for w in range(window):
            summed = jnp.zeros((blk, blk), jnp.float32)
            for k in range(slots):
                keep = ((local[k] == w) & (count > k)).astype(jnp.float32)
                summed += T[b, k].astype(jnp.float32) * keep
            E[g, at, w * blk : (w + 1) * blk] = summed.astype(jnp.bfloat16)
        return carry

    lax.fori_loop(0, blocks, densify, 0)

    for role in (1, 2):
        @pl.when(g == role)
        def _():
            for j in WHOLE_WEIGHTS[role]:
                begin(role, whole, role, j)
            for b in range(blocks):
                begin(role, own, role, role - 1, MATS + b)
                if b == 0:
                    begin(role, own, role, 2 - role, MATS)
            if not (RELAY_FIRST and role in RELAYS):
                for b in range(1, blocks):
                    begin(role, own, role, 2 - role, MATS + b)

    for copy in copies[2:]:
        copy.wait()

    def run(role, keys):
        for kind, s, j in keys:
            if kind == "x":
                forward(s, j, 0).wait_recv()
                begin(role, to_core, s, j, 0)
                if role != 0 or j not in WHOLE_WEIGHTS.get(s, ()):
                    begin(role, to_pair, s, j)
                to = weight_target(role, s, j)
                if to is not None:
                    begin(role, forward, s, j, to)
                if role == 3:
                    other = 3 - s
                    side = (other ^ role) - 1
                    if j < 2:
                        begin(role, own, role, side, j + 2)
                    if j == 3:
                        for b in BLOCK_ORDER[other]:
                            begin(role, own, role, side, MATS + b)
            elif kind == "z":
                wait_pair(s, j)
                begin(role, to_core, s, j, 1)
            elif kind == "e":
                wait_block(s, j)
                begin(role, forward, s, MATS + j, edge_target(role, s, j))
            else:
                for k in ((0, 1), (2,))[j]:
                    ref = state_part(sections - 1, k)
                    remote(ref, ref, sr.at[k], rr.at[k], (g, cd)).wait_recv()
                    begin(role, relay, k)
                if RELAY_FIRST and j == max(h for h in range(2) if RELAYS[h] == role):
                    for b in range(1, blocks):
                        begin(role, own, role, 2 - role, MATS + b)

    def poll(u, p, among):
        for role in roles:
            for (unit, piece), keys in ORDER[role].items():
                if piece == p and unit in among:
                    pl.when((g == role) & (u == unit))(functools.partial(run, role, keys))

    def wait_blocks(s, which):
        for b in which:
            passed = jnp.bool_(False)
            for role in roles:
                for section in roles[1:]:
                    if section != role and edge_target(role, section, b) is not None:
                        passed = passed | ((g == role) & (s == section))
            pl.when(jnp.logical_not(passed))(functools.partial(wait_block, s, b))

    def section_of(u):
        return jnp.maximum(u - (sections - 1), 0)

    def first_senders(u):
        s = section_of(u)

        @pl.when(s != g)
        def _():
            wait_core(s, 0)

        outer_senders(u, s, g)

    def update(edges, base, s, u, state):
        gathered = jnp.dot(edges, PAD[u], preferred_element_type=jnp.float32)
        mixed = base + jnp.dot(
            gathered.astype(jnp.bfloat16), W[s, 2], preferred_element_type=jnp.float32
        )
        scale = lax.rsqrt(jnp.mean(mixed * mixed, axis=-1, keepdims=True) + 1e-05)
        change = silu(mixed * scale * G[s]).astype(jnp.bfloat16)
        result = state.astype(jnp.float32) + jnp.dot(
            change, W[s, 3], preferred_element_type=jnp.float32
        )
        return result.astype(jnp.bfloat16)

    def send_state(u, parts):
        for unit in range(sections - 1):
            @pl.when((g == 0) & (u == unit))
            def _():
                for k in parts:
                    begin(0, state, sections - 1 - unit, k)

        @pl.when(u == units - 1)
        def _():
            for k in parts:
                out_copy(k).start()

    def out_copy(k):
        at = (pl.ds(0, halo), pl.ds(rows - halo, halo), pl.ds(halo, rows - 2 * halo))[k]
        return pltpu.make_async_copy(H.at[g, at], out_ref.at[0, at], so.at[k])

    every = range(units)

    def unit_body(u, carry):
        s = section_of(u)
        n = jnp.where(u < sections, sections - 1 - u, g)
        active = (u >= sections) | (g == 0)
        fetched = s != g

        poll(u, 0, (sections,))

        @pl.when(u == sections)
        def _():
            @pl.when(g != 0)
            def _():
                for k in range(2):
                    wait_state(g, k)

            first_senders(u)

        poll(u, 1, every)

        @pl.when(active)
        def _():
            @pl.when((u == sections) & (g != 0))
            def _():
                wait_state(g, 2)

            @pl.when(u >= sections)
            def _():
                inner_senders(u, s, n)

            @pl.when(fetched)
            def _():
                wait_core(s, 1)

            for i in range(2):
                at = pl.ds(i * half, half)
                BASE[at] = jnp.dot(H[n, at], W[s, 1], preferred_element_type=jnp.float32)

        poll(u, 2, every)

        @pl.when(active)
        def _():
            @pl.when(fetched)
            def _():
                wait_core(s, 2)
                wait_core(s, 3)
                wait_gain(s)
                wait_blocks(s, [*range(HB), *range(blocks - HB, blocks)])

            for copy in halos(u):
                copy.wait_recv()
            result = update(outer(E, s), outer(BASE), s, u, outer(H, n))
            H[n, :halo] = result[:halo]
            H[n, rows - halo : rows] = result[halo:]
            send_state(u, (0, 1))

        poll(u + 1, 0, range(sections + 1, units))

        @pl.when((u >= sections) & (u < units - 1))
        def _():
            first_senders(u + 1)

        poll(u, 3, every)

        @pl.when(active)
        def _():
            @pl.when(fetched)
            def _():
                wait_blocks(s, range(HB, blocks - HB))

            at = pl.ds(halo, rows - 2 * halo)
            H[n, at] = update(E[s, at], BASE[at], s, u, H[n, at])
            send_state(u, (2,))
            for copy in halos(u):
                copy.wait_send()

        return carry

    lax.fori_loop(0, units, unit_body, 0)

    for role in roles:
        @pl.when(g == role)
        def _():
            run(role, ORDER[role][-1, 0])
            for make, args in started[role]:
                make(*args).wait_send()

    for k in range(3):
        out_copy(k).wait()


def shards(
    sections, domains,
    samples, w_source, w_self, w_message, w_output, norm_gain, tile_source, tile_count, tile_value,
):
    _, blocks, slots, blk, _ = tile_value.shape
    rows, width = samples.shape[1:]
    window = blocks + 2 * HB
    units = 2 * sections - 1
    chunks = MATS + blocks
    dma = pltpu.SemaphoreType.DMA
    anywhere = pl.BlockSpec(memory_space=pl.ANY)
    scalars = pl.BlockSpec(memory_space=pltpu.SMEM)
    flops = 2 * rows * width * (MATS * width + window * blk) * sections
    return pl.pallas_call(
        functools.partial(kernel, sections, domains),
        out_shape=jax.ShapeDtypeStruct((1, rows, width), jnp.bfloat16),
        in_specs=[scalars] * 2 + [anywhere] * 7,
        out_specs=anywhere,
        scratch_shapes=[
            pltpu.VMEM((sections, MATS, width, width), jnp.bfloat16),
            pltpu.VMEM((sections, rows, window * blk), jnp.bfloat16),
            pltpu.VMEM((sections, 1, width), jnp.float32),
            pltpu.VMEM((blocks, slots, blk, blk), jnp.bfloat16),
            pltpu.VMEM((sections, rows, width), jnp.bfloat16),
            pltpu.VMEM((units, window * blk, width), jnp.bfloat16),
            pltpu.VMEM((rows, width), jnp.float32),
            dma((MATS + 3,)),
            dma((sections, chunks)),
            dma((sections, MATS)),
            dma((sections, MATS, 2)),
            dma((sections,)),
            dma((3,)),
            dma((3,)),
            dma((units, 2)),
            dma((2, chunks)),
            dma((sections, chunks)),
            dma((sections, MATS)),
            dma((sections, MATS, 2)),
            dma((3,)),
            dma((sections, 3)),
            dma((3,)),
            dma((units, 2)),
            dma((3,)),
        ],
        compiler_params=pltpu.CompilerParams(
            collective_id=0, has_side_effects=True, vmem_limit_bytes=60 * 2**20
        ),
        cost_estimate=pl.CostEstimate(flops=flops, bytes_accessed=flops // 128, transcendentals=0),
    )(
        tile_source, tile_count, samples, w_source, w_self, w_message, w_output, norm_gain, tile_value
    )


def solution(mesh):
    return jax.shard_map(
        functools.partial(shards, mesh.shape["segment"], mesh.shape["dom"]),
        mesh=mesh,
        in_specs=(
            P(None, "dom", None),
            P("segment", None, None, None),
            P("segment", None, None, None),
            P("segment", None, None, None),
            P("segment", None, None, None),
            P("segment", None, None),
            P("segment", "dom", None),
            P("segment", "dom"),
            P("segment", "dom", None, None, None),
        ),
        out_specs=P("segment", "dom", None),
        check_vma=False,
    )
```

```python
import functools

import jax
import jax.numpy as jnp
from jax import lax
from jax.experimental import pallas as pl
from jax.experimental.pallas import tpu as pltpu
from jax.sharding import PartitionSpec as P

HB = 1
MESH = pl.DeviceIdType.MESH
MATS = 4

EDGES_BY_LAST = {1: [0, 1], 2: []}
WEIGHTS_BY_FIRST = {1: [0, 3], 2: []}
WHOLE_WEIGHTS = {1: [], 2: [0, 1, 3]}
BLOCKS_BY_ONE = 2
BLOCK_ORDER = {2: [1, 2, 3, 0], 1: [1, 2, 0, 3]}
RELAYS = (1, 2)
RELAY_FIRST = True
ORDER = {
    0: {
        (0, 2): [('x', 1, 0), ('x', 1, 1)],
        (1, 3): [('x', 1, 2)],
        (2, 1): [('x', 1, 3)],
        (2, 2): [('x', 2, 3)],
        (3, 1): [('z', 2, 0)],
        (4, 0): [('z', 1, 0), ('x', 2, 1)],
        (4, 1): [('z', 2, 1), ('x', 2, 0), ('x', 2, 2), ('z', 2, 3), ('z', 1, 2), ('z', 1, 1)],
        (4, 2): [('e', 2, 0), ('z', 1, 3), ('e', 1, 3)],
        (4, 3): [('x', 3, 0), ('z', 2, 2), ('e', 2, 2), ('x', 3, 1), ('e', 2, 3), ('e', 1, 2)],
        (5, 1): [('e', 2, 1), ('x', 3, 2)],
        (5, 2): [('z', 3, 0)],
        (6, 0): [('x', 3, 3)],
        (6, 1): [('z', 3, 1)],
        (6, 2): [('z', 3, 2), ('z', 3, 3)],
        (-1, 0): [],
    },
    1: {
        (4, 0): [('x', 3, 0), ('x', 2, 0), ('z', 3, 0), ('x', 3, 1), ('r', 3, 0), ('z', 3, 1), ('x', 3, 2), ('x', 2, 2), ('z', 3, 2)],
        (4, 1): [('x', 2, 1), ('x', 3, 3), ('e', 3, 1)],
        (4, 2): [('x', 2, 3), ('z', 2, 0), ('z', 2, 2)],
        (5, 0): [('z', 3, 3)],
        (5, 1): [('e', 3, 0), ('z', 2, 1)],
        (5, 2): [('z', 2, 3)],
        (-1, 0): [],
    },
    2: {
        (4, 0): [('x', 3, 1), ('x', 3, 2), ('x', 3, 0), ('z', 3, 1), ('x', 1, 1), ('z', 3, 2), ('x', 1, 0), ('r', 3, 1), ('x', 1, 2), ('x', 3, 3), ('z', 1, 0)],
        (4, 1): [('z', 1, 1)],
        (4, 2): [('z', 1, 2), ('z', 3, 3), ('e', 3, 2), ('x', 1, 3), ('z', 3, 0), ('e', 3, 3), ('z', 1, 3)],
        (-1, 0): [],
    },
    3: {
        (4, 0): [('x', 1, 0), ('x', 2, 0), ('x', 1, 1), ('x', 1, 2), ('x', 2, 2), ('x', 2, 1), ('x', 2, 3), ('z', 1, 1), ('e', 1, 0), ('z', 2, 0), ('x', 1, 3), ('z', 1, 0)],
        (4, 2): [('z', 1, 2), ('e', 1, 1), ('z', 1, 3), ('z', 2, 1), ('z', 2, 2)],
        (5, 1): [('z', 2, 3)],
        (-1, 0): [],
    },
}


def edge_target(role, section, block):
    if section in EDGES_BY_LAST and role in (0, 3):
        if (block in EDGES_BY_LAST[section]) == (role == 3):
            return 3 - section
    if section == 3 and role == (1 if block < BLOCKS_BY_ONE else 2):
        return 0
    return None


def weight_target(role, section, j):
    if section in WEIGHTS_BY_FIRST and role in (0, 3):
        if (j in WEIGHTS_BY_FIRST[section]) == (role == 0):
            return 3 - section
    if role == 1 and section == 3:
        return 0
    return None


def silu(v):
    half = 0.5 * v
    return half + half * jnp.tanh(half)


def kernel(
    sections, domains,
    source_ref, count_ref, samples_ref, wa_ref, wb_ref, wc_ref, wd_ref, gain_ref, tiles_ref,
    out_ref,
    W, E, G, T, H, PAD, BASE,
    l_sem, rx, rz, rc, rg, ra, rr, rh, sx, sf, sz, sc, sg, sa, sr, sh, so,
):
    g = lax.axis_index("segment")
    d = lax.axis_index("dom")
    w_refs = (wa_ref, wb_ref, wc_ref, wd_ref)
    _, blocks, slots, blk, _ = tiles_ref.shape
    window = blocks + 2 * HB
    rows = blocks * blk
    halo = HB * blk
    width = samples_ref.shape[-1]
    quarter = width // 4
    half = rows // 2
    per_half = blocks // 2
    units = 2 * sections - 1
    roles = range(sections)
    q = lax.rem(d, 4)
    zd = d + 2 - 4 * (q // 2)
    cd = d + 1 - 2 * lax.rem(d, 2)
    nxt, prv = lax.rem(d + 1, domains), lax.rem(d + domains - 1, domains)
    zq = lax.rem(zd, 4)
    cq = lax.rem(cd, 4)
    czq = lax.rem(q + 1 - 2 * lax.rem(q, 2) + 2, 4)

    def part(index):
        return pl.ds(pl.multiple_of(index * quarter, quarter), quarter)

    def remote(src, dst, send, recv, device):
        return pltpu.make_async_remote_copy(
            src_ref=src, dst_ref=dst, send_sem=send, recv_sem=recv,
            device_id=device, device_id_type=MESH,
        )

    def piece_of(s, j):
        if j < MATS:
            return W.at[s, j, part(q)]
        return E.at[s, pl.ds((j - MATS) * blk, blk)]

    def own(role, side, j):
        src = w_refs[j].at[0, 0, part(q)] if j < MATS else piece_of(role, j)
        to = role ^ (1 + side)
        return remote(src, piece_of(role, j), sx.at[side, j], rx.at[role, j], (to, d))

    def forward(s, j, to):
        return remote(piece_of(s, j), piece_of(s, j), sf.at[s, j], rx.at[s, j], (to, d))

    def to_pair(s, j):
        return remote(W.at[s, j, part(q)], W.at[s, j, part(q)], sz.at[s, j], rz.at[s, j], (g, zd))

    def to_core(s, j, kind):
        at = part(zq if kind else q)
        return remote(W.at[s, j, at], W.at[s, j, at], sc.at[s, j, kind], rc.at[s, j, kind], (g, cd))

    def wait_pair(s, j):
        remote(W.at[s, j, part(zq)], W.at[s, j, part(zq)], sz.at[s, j], rz.at[s, j], (g, zd)).wait_recv()

    def wait_core(s, j):
        for kind, index in enumerate((cq, czq)):
            at = part(index)
            remote(W.at[s, j, at], W.at[s, j, at], sc.at[s, j, kind], rc.at[s, j, kind], (g, cd)).wait_recv()

    def wait_block(s, b):
        at = pl.ds(b * blk, blk)
        remote(E.at[s, at], E.at[s, at], sf.at[s, MATS + b], rx.at[s, MATS + b], (g, cd)).wait_recv()

    def gain(role, k):
        to = role ^ (1 + k)
        return remote(gain_ref.at[pl.ds(0, 1)], G.at[pl.ds(role, 1)], sg.at[k], rg.at[role], (to, d))

    def wait_gain(s):
        remote(gain_ref.at[pl.ds(0, 1)], G.at[pl.ds(s, 1)], sg.at[0], rg.at[s], (g, cd)).wait_recv()

    def state_part(n, k):
        at = (pl.ds(0, halo), pl.ds(rows - halo, halo), pl.ds(halo, rows - 2 * halo))[k]
        return H.at[n, at]

    def state(n, k):
        last = sections - 1
        ref = state_part(n, k)
        if n == last:
            return remote(ref, ref, sa.at[n, k], rr.at[k], (RELAYS[k // 2], d))
        return remote(ref, ref, sa.at[n, k], ra.at[k], (n, d))

    def relay(k):
        last = sections - 1
        ref = state_part(last, k)
        return remote(ref, ref, sr.at[k], ra.at[k], (last, d))

    def wait_state(n, k):
        ref = state_part(n, k)
        remote(ref, ref, sr.at[k], ra.at[k], (g, cd)).wait_recv()

    def whole(role, j):
        at = part(zq)
        src = w_refs[j].at[0, 0, at]
        return remote(src, W.at[role, j, at], sz.at[role, j], rz.at[role, j], (0, d))

    def halos(u):
        first = PAD.at[u, pl.ds(halo, halo)]
        final = PAD.at[u, pl.ds(rows, halo)]
        return (
            remote(final, PAD.at[u, pl.ds(0, halo)], sh.at[u, 0], rh.at[u, 0], (g, nxt)),
            remote(first, PAD.at[u, pl.ds(halo + rows, halo)], sh.at[u, 1], rh.at[u, 1], (g, prv)),
        )

    def local_copies():
        made = [pltpu.make_async_copy(tiles_ref.at[0], T, l_sem.at[0])]
        made += [
            pltpu.make_async_copy(w_refs[j].at[0, 0], W.at[g, j], l_sem.at[1 + j]) for j in range(MATS)
        ]
        made.append(
            pltpu.make_async_copy(gain_ref.at[pl.ds(0, 1)], G.at[pl.ds(g, 1)], l_sem.at[1 + MATS])
        )
        return made

    samples_copy = pltpu.make_async_copy(samples_ref, H, l_sem.at[2 + MATS])

    for copy in local_copies():
        copy.start()

    @pl.when(g == 0)
    def _():
        samples_copy.start()

    barrier = pltpu.get_barrier_semaphore()
    peers = [(lax.rem(g + k, sections), d) for k in range(1, sections)]
    peers += [(g, zd), (g, cd), (g, nxt), (g, prv)]
    for peer in peers:
        pl.semaphore_signal(barrier, inc=1, device_id=peer, device_id_type=MESH)
    copies = local_copies()

    def outer(ref, *index):
        return jnp.concatenate([ref[*index, :halo], ref[*index, rows - halo : rows]])

    def outer_senders(u, s, n):
        v = jnp.dot(outer(H, n), W[s, 0], preferred_element_type=jnp.float32)
        v = silu(v).astype(jnp.bfloat16)
        PAD[u, halo : 2 * halo] = v[:halo]
        PAD[u, rows : rows + halo] = v[halo:]

    def inner_senders(u, s, n):
        v = jnp.dot(H[n, halo : rows - halo], W[s, 0], preferred_element_type=jnp.float32)
        PAD[u, 2 * halo : rows] = silu(v).astype(jnp.bfloat16)

    def home_senders(u, carry):
        outer_senders(u, 0, sections - 1 - u)
        inner_senders(u, 0, sections - 1 - u)
        return carry

    @pl.when(g == 0)
    def _():
        copies[1].wait()
        samples_copy.wait()
        lax.fori_loop(0, sections, home_senders, 0)

    pl.semaphore_wait(barrier, len(peers))

    @pl.when(g == 0)
    def _():
        for u in range(sections):
            for copy in halos(u):
                copy.start()

    started = {role: [] for role in roles}

    def begin(role, make, *args):
        make(*args).start()
        started[role].append((make, args))

    for role in roles[1:]:
        @pl.when(g == role)
        def _():
            for j in range(MATS if role < 3 else 2):
                for side in range(2):
                    begin(role, own, role, side, j)
            for k in range(3):
                begin(role, gain, role, k)

    copies[0].wait()
    total = blocks * domains
    base = d * blocks - HB

    def densify(b, carry):
        local = [lax.rem(source_ref[0, b, k] - base + total, total) for k in range(slots)]
        count = count_ref[0, b]
        at = pl.ds(pl.multiple_of(b * blk, blk), blk)
        for w in range(window):
            summed = jnp.zeros((blk, blk), jnp.float32)
            for k in range(slots):
                keep = ((local[k] == w) & (count > k)).astype(jnp.float32)
                summed += T[b, k].astype(jnp.float32) * keep
            E[g, at, w * blk : (w + 1) * blk] = summed.astype(jnp.bfloat16)
        return carry

    lax.fori_loop(0, blocks, densify, 0)

    for role in (1, 2):
        @pl.when(g == role)
        def _():
            for j in WHOLE_WEIGHTS[role]:
                begin(role, whole, role, j)
            for b in range(blocks):
                begin(role, own, role, role - 1, MATS + b)
                if b == 0:
                    begin(role, own, role, 2 - role, MATS)
            if not (RELAY_FIRST and role in RELAYS):
                for b in range(1, blocks):
                    begin(role, own, role, 2 - role, MATS + b)

    @pl.when(g != 0)
    def _():
        copies[1].wait()

    for copy in copies[2:]:
        copy.wait()

    def run(role, keys):
        for kind, s, j in keys:
            if kind == "x":
                forward(s, j, 0).wait_recv()
                begin(role, to_core, s, j, 0)
                if role != 0 or j not in WHOLE_WEIGHTS.get(s, ()):
                    begin(role, to_pair, s, j)
                to = weight_target(role, s, j)
                if to is not None:
                    begin(role, forward, s, j, to)
                if role == 3:
                    other = 3 - s
                    side = (other ^ role) - 1
                    if j < 2:
                        begin(role, own, role, side, j + 2)
                    if j == 3:
                        for b in BLOCK_ORDER[other]:
                            begin(role, own, role, side, MATS + b)
            elif kind == "z":
                wait_pair(s, j)
                begin(role, to_core, s, j, 1)
            elif kind == "e":
                wait_block(s, j)
                begin(role, forward, s, MATS + j, edge_target(role, s, j))
            else:
                for k in ((0, 1), (2,))[j]:
                    ref = state_part(sections - 1, k)
                    remote(ref, ref, sr.at[k], rr.at[k], (g, cd)).wait_recv()
                    begin(role, relay, k)
                if RELAY_FIRST and j == max(h for h in range(2) if RELAYS[h] == role):
                    for b in range(1, blocks):
                        begin(role, own, role, 2 - role, MATS + b)

    def poll(u, p, among):
        for role in roles:
            for (unit, piece), keys in ORDER[role].items():
                if piece == p and unit in among:
                    pl.when((g == role) & (u == unit))(functools.partial(run, role, keys))

    def wait_blocks(s, which):
        for b in which:
            passed = jnp.bool_(False)
            for role in roles:
                for section in roles[1:]:
                    if section != role and edge_target(role, section, b) is not None:
                        passed = passed | ((g == role) & (s == section))
            pl.when(jnp.logical_not(passed))(functools.partial(wait_block, s, b))

    def section_of(u):
        return jnp.maximum(u - (sections - 1), 0)

    def first_senders(u):
        s = section_of(u)

        @pl.when(s != g)
        def _():
            wait_core(s, 0)

        outer_senders(u, s, g)
        for copy in halos(u):
            copy.start()

    def inside(edges, u):
        return jnp.dot(
            edges[:, halo : halo + rows], PAD[u, halo : halo + rows], preferred_element_type=jnp.float32
        )

    def outside(edges, u):
        beside = jnp.concatenate([edges[:, :halo], edges[:, halo + rows :]], axis=1)
        read = jnp.concatenate([PAD[u, :halo], PAD[u, halo + rows :]])
        return jnp.dot(beside, read, preferred_element_type=jnp.float32)

    def update(gathered, base, s, u, state):
        mixed = base + jnp.dot(
            gathered.astype(jnp.bfloat16), W[s, 2], preferred_element_type=jnp.float32
        )
        scale = lax.rsqrt(jnp.mean(mixed * mixed, axis=-1, keepdims=True) + 1e-05)
        change = silu(mixed * scale * G[s]).astype(jnp.bfloat16)
        result = state.astype(jnp.float32) + jnp.dot(
            change, W[s, 3], preferred_element_type=jnp.float32
        )
        return result.astype(jnp.bfloat16)

    def send_state(u, parts):
        for unit in range(sections - 1):
            @pl.when((g == 0) & (u == unit))
            def _():
                for k in parts:
                    begin(0, state, sections - 1 - unit, k)

        @pl.when(u == units - 1)
        def _():
            for k in parts:
                out_copy(k).start()

    def out_copy(k):
        at = (pl.ds(0, halo), pl.ds(rows - halo, halo), pl.ds(halo, rows - 2 * halo))[k]
        return pltpu.make_async_copy(H.at[g, at], out_ref.at[0, at], so.at[k])

    every = range(units)

    def unit_body(u, carry):
        s = section_of(u)
        n = jnp.where(u < sections, sections - 1 - u, g)
        active = (u >= sections) | (g == 0)
        fetched = s != g

        poll(u, 0, (sections,))

        @pl.when(u == sections)
        def _():
            @pl.when(g != 0)
            def _():
                for k in range(2):
                    wait_state(g, k)

            first_senders(u)

        poll(u, 1, every)

        @pl.when(active)
        def _():
            @pl.when((u == sections) & (g != 0))
            def _():
                wait_state(g, 2)

            @pl.when(u >= sections)
            def _():
                inner_senders(u, s, n)

            @pl.when(fetched)
            def _():
                wait_core(s, 1)

            for i in range(2):
                at = pl.ds(i * half, half)
                BASE[at] = jnp.dot(H[n, at], W[s, 1], preferred_element_type=jnp.float32)

        poll(u, 2, every)

        @pl.when(active)
        def _():
            @pl.when(fetched)
            def _():
                wait_core(s, 2)
                wait_core(s, 3)
                wait_gain(s)
                wait_blocks(s, [*range(HB), *range(blocks - HB, blocks)])

            gathered = inside(outer(E, s), u)
            for copy in halos(u):
                copy.wait_recv()
            gathered += outside(outer(E, s), u)
            result = update(gathered, outer(BASE), s, u, outer(H, n))
            H[n, :halo] = result[:halo]
            H[n, rows - halo : rows] = result[halo:]
            send_state(u, (0, 1))

        poll(u + 1, 0, range(sections + 1, units))

        @pl.when((u >= sections) & (u < units - 1))
        def _():
            first_senders(u + 1)

        poll(u, 3, every)

        @pl.when(active)
        def _():
            @pl.when(fetched)
            def _():
                wait_blocks(s, range(HB, blocks - HB))

            at = pl.ds(halo, rows - 2 * halo)
            gathered = jnp.dot(E[s, at], PAD[u], preferred_element_type=jnp.float32)
            H[n, at] = update(gathered, BASE[at], s, u, H[n, at])
            send_state(u, (2,))
            for copy in halos(u):
                copy.wait_send()

        return carry

    lax.fori_loop(0, units, unit_body, 0)

    for role in roles:
        @pl.when(g == role)
        def _():
            run(role, ORDER[role][-1, 0])
            for make, args in started[role]:
                make(*args).wait_send()

    for k in range(3):
        out_copy(k).wait()


def shards(
    sections, domains,
    samples, w_source, w_self, w_message, w_output, norm_gain, tile_source, tile_count, tile_value,
):
    _, blocks, slots, blk, _ = tile_value.shape
    rows, width = samples.shape[1:]
    window = blocks + 2 * HB
    units = 2 * sections - 1
    chunks = MATS + blocks
    dma = pltpu.SemaphoreType.DMA
    anywhere = pl.BlockSpec(memory_space=pl.ANY)
    scalars = pl.BlockSpec(memory_space=pltpu.SMEM)
    flops = 2 * rows * width * (MATS * width + window * blk) * sections
    return pl.pallas_call(
        functools.partial(kernel, sections, domains),
        out_shape=jax.ShapeDtypeStruct((1, rows, width), jnp.bfloat16),
        in_specs=[scalars] * 2 + [anywhere] * 7,
        out_specs=anywhere,
        scratch_shapes=[
            pltpu.VMEM((sections, MATS, width, width), jnp.bfloat16),
            pltpu.VMEM((sections, rows, window * blk), jnp.bfloat16),
            pltpu.VMEM((sections, 1, width), jnp.float32),
            pltpu.VMEM((blocks, slots, blk, blk), jnp.bfloat16),
            pltpu.VMEM((sections, rows, width), jnp.bfloat16),
            pltpu.VMEM((units, window * blk, width), jnp.bfloat16),
            pltpu.VMEM((rows, width), jnp.float32),
            dma((MATS + 3,)),
            dma((sections, chunks)),
            dma((sections, MATS)),
            dma((sections, MATS, 2)),
            dma((sections,)),
            dma((3,)),
            dma((3,)),
            dma((units, 2)),
            dma((2, chunks)),
            dma((sections, chunks)),
            dma((sections, MATS)),
            dma((sections, MATS, 2)),
            dma((3,)),
            dma((sections, 3)),
            dma((3,)),
            dma((units, 2)),
            dma((3,)),
        ],
        compiler_params=pltpu.CompilerParams(
            collective_id=0, has_side_effects=True, vmem_limit_bytes=60 * 2**20
        ),
        cost_estimate=pl.CostEstimate(flops=flops, bytes_accessed=flops // 128, transcendentals=0),
    )(
        tile_source, tile_count, samples, w_source, w_self, w_message, w_output, norm_gain, tile_value
    )


def solution(mesh):
    return jax.shard_map(
        functools.partial(shards, mesh.shape["segment"], mesh.shape["dom"]),
        mesh=mesh,
        in_specs=(
            P(None, "dom", None),
            P("segment", None, None, None),
            P("segment", None, None, None),
            P("segment", None, None, None),
            P("segment", None, None, None),
            P("segment", None, None),
            P("segment", "dom", None),
            P("segment", "dom"),
            P("segment", "dom", None, None, None),
        ),
        out_specs=P("segment", "dom", None),
        check_vma=False,
    )
```

```python
import functools

import jax
import jax.numpy as jnp
from jax import lax
from jax.experimental import pallas as pl
from jax.experimental.pallas import tpu as pltpu
from jax.sharding import PartitionSpec as P

HB = 1
MESH = pl.DeviceIdType.MESH
MATS = 4

EDGES_BY_LAST = {1: [0, 1], 2: []}
WEIGHTS_BY_FIRST = {1: [0, 3], 2: []}
WHOLE_WEIGHTS = {1: [], 2: [0, 1, 3]}
BLOCKS_BY_ONE = 2
BLOCK_ORDER = {2: [1, 2, 3, 0], 1: [1, 2, 0, 3]}
RELAYS = (1, 2)
WEIGHTS_BY_TWO = []
RELAY_FIRST = True
ORDER = {
    0: {
        (0, 2): [('x', 1, 0), ('x', 1, 1)],
        (1, 3): [('x', 1, 2)],
        (2, 1): [('x', 1, 3)],
        (2, 2): [('x', 2, 3)],
        (3, 1): [('z', 2, 0)],
        (4, 0): [('z', 1, 0), ('x', 2, 1)],
        (4, 1): [('z', 2, 1), ('x', 2, 0), ('x', 2, 2), ('z', 2, 3), ('z', 1, 2), ('z', 1, 1)],
        (4, 2): [('e', 2, 0), ('z', 1, 3), ('e', 1, 3)],
        (4, 3): [('x', 3, 0), ('z', 2, 2), ('e', 2, 2), ('x', 3, 1), ('e', 1, 2)],
        (5, 1): [('e', 2, 3), ('e', 2, 1), ('x', 3, 2)],
        (5, 2): [('z', 3, 0)],
        (6, 0): [('x', 3, 3)],
        (6, 1): [('z', 3, 1)],
        (6, 2): [('z', 3, 2), ('z', 3, 3)],
        (-1, 0): [],
    },
    1: {
        (4, 0): [('x', 3, 0), ('x', 2, 0), ('z', 3, 0), ('x', 3, 1), ('r', 3, 0), ('z', 3, 1), ('x', 3, 2), ('x', 2, 2), ('z', 2, 2), ('z', 3, 2)],
        (4, 1): [('x', 2, 1), ('x', 3, 3), ('e', 3, 1)],
        (4, 2): [('x', 2, 3), ('z', 2, 0)],
        (5, 0): [('z', 3, 3)],
        (5, 1): [('e', 3, 0), ('z', 2, 1)],
        (5, 2): [('z', 2, 3)],
        (-1, 0): [],
    },
    2: {
        (4, 0): [('x', 3, 1), ('x', 3, 2), ('x', 3, 0), ('z', 3, 1), ('x', 1, 1), ('z', 3, 2), ('x', 1, 0), ('r', 3, 1), ('x', 1, 2), ('x', 3, 3), ('z', 1, 1), ('z', 1, 0)],
        (4, 2): [('z', 1, 2), ('z', 3, 3), ('e', 3, 2), ('x', 1, 3), ('z', 1, 3), ('z', 3, 0), ('e', 3, 3)],
        (-1, 0): [],
    },
    3: {
        (4, 0): [('x', 1, 0), ('x', 2, 0), ('x', 1, 1), ('x', 1, 2), ('x', 2, 2), ('x', 2, 1), ('x', 2, 3), ('z', 1, 1), ('e', 1, 0), ('z', 2, 0), ('x', 1, 3), ('z', 1, 0)],
        (4, 2): [('z', 1, 2), ('e', 1, 1), ('z', 1, 3), ('z', 2, 1), ('z', 2, 2)],
        (5, 1): [('z', 2, 3)],
        (-1, 0): [],
    },
}


def edge_target(role, section, block):
    if section in EDGES_BY_LAST and role in (0, 3):
        if (block in EDGES_BY_LAST[section]) == (role == 3):
            return 3 - section
    if section == 3 and role == (1 if block < BLOCKS_BY_ONE else 2):
        return 0
    return None


def weight_target(role, section, j):
    if section in WEIGHTS_BY_FIRST and role in (0, 3):
        if (j in WEIGHTS_BY_FIRST[section]) == (role == 0):
            return 3 - section
    if section == 3 and role == (2 if j in WEIGHTS_BY_TWO else 1):
        return 0
    return None


def silu(v):
    half = 0.5 * v
    return half + half * jnp.tanh(half)


def kernel(
    sections, domains,
    source_ref, count_ref, samples_ref, wa_ref, wb_ref, wc_ref, wd_ref, gain_ref, tiles_ref,
    out_ref,
    W, E, G, T, H, PAD, BASE,
    l_sem, rx, rz, rc, rg, ra, rr, rh, sx, sf, sz, sc, sg, sa, sr, sh, so,
):
    g = lax.axis_index("segment")
    d = lax.axis_index("dom")
    w_refs = (wa_ref, wb_ref, wc_ref, wd_ref)
    _, blocks, slots, blk, _ = tiles_ref.shape
    window = blocks + 2 * HB
    rows = blocks * blk
    halo = HB * blk
    width = samples_ref.shape[-1]
    quarter = width // 4
    half = rows // 2
    per_half = blocks // 2
    units = 2 * sections - 1
    roles = range(sections)
    q = lax.rem(d, 4)
    zd = d + 2 - 4 * (q // 2)
    cd = d + 1 - 2 * lax.rem(d, 2)
    nxt, prv = lax.rem(d + 1, domains), lax.rem(d + domains - 1, domains)
    zq = lax.rem(zd, 4)
    cq = lax.rem(cd, 4)
    czq = lax.rem(q + 1 - 2 * lax.rem(q, 2) + 2, 4)

    def part(index):
        return pl.ds(pl.multiple_of(index * quarter, quarter), quarter)

    def remote(src, dst, send, recv, device):
        return pltpu.make_async_remote_copy(
            src_ref=src, dst_ref=dst, send_sem=send, recv_sem=recv,
            device_id=device, device_id_type=MESH,
        )

    def piece_of(s, j):
        if j < MATS:
            return W.at[s, j, part(q)]
        return E.at[s, pl.ds((j - MATS) * blk, blk)]

    def own(role, side, j):
        src = w_refs[j].at[0, 0, part(q)] if j < MATS else piece_of(role, j)
        to = role ^ (1 + side)
        return remote(src, piece_of(role, j), sx.at[side, j], rx.at[role, j], (to, d))

    def forward(s, j, to):
        return remote(piece_of(s, j), piece_of(s, j), sf.at[s, j], rx.at[s, j], (to, d))

    def to_pair(s, j):
        return remote(W.at[s, j, part(q)], W.at[s, j, part(q)], sz.at[s, j], rz.at[s, j], (g, zd))

    def to_core(s, j, kind):
        at = part(zq if kind else q)
        return remote(W.at[s, j, at], W.at[s, j, at], sc.at[s, j, kind], rc.at[s, j, kind], (g, cd))

    def wait_pair(s, j):
        remote(W.at[s, j, part(zq)], W.at[s, j, part(zq)], sz.at[s, j], rz.at[s, j], (g, zd)).wait_recv()

    def wait_core(s, j):
        for kind, index in enumerate((cq, czq)):
            at = part(index)
            remote(W.at[s, j, at], W.at[s, j, at], sc.at[s, j, kind], rc.at[s, j, kind], (g, cd)).wait_recv()

    def wait_block(s, b):
        at = pl.ds(b * blk, blk)
        remote(E.at[s, at], E.at[s, at], sf.at[s, MATS + b], rx.at[s, MATS + b], (g, cd)).wait_recv()

    def gain(role, k):
        to = role ^ (1 + k)
        return remote(gain_ref.at[pl.ds(0, 1)], G.at[pl.ds(role, 1)], sg.at[k], rg.at[role], (to, d))

    def wait_gain(s):
        remote(gain_ref.at[pl.ds(0, 1)], G.at[pl.ds(s, 1)], sg.at[0], rg.at[s], (g, cd)).wait_recv()

    def state_part(n, k):
        at = (pl.ds(0, halo), pl.ds(rows - halo, halo), pl.ds(halo, rows - 2 * halo))[k]
        return H.at[n, at]

    def state(n, k):
        last = sections - 1
        ref = state_part(n, k)
        if n == last:
            return remote(ref, ref, sa.at[n, k], rr.at[k], (RELAYS[k // 2], d))
        return remote(ref, ref, sa.at[n, k], ra.at[k], (n, d))

    def relay(k):
        last = sections - 1
        ref = state_part(last, k)
        return remote(ref, ref, sr.at[k], ra.at[k], (last, d))

    def wait_state(n, k):
        ref = state_part(n, k)
        remote(ref, ref, sr.at[k], ra.at[k], (g, cd)).wait_recv()

    def whole(role, j):
        at = part(zq)
        src = w_refs[j].at[0, 0, at]
        return remote(src, W.at[role, j, at], sz.at[role, j], rz.at[role, j], (0, d))

    def halos(u):
        first = PAD.at[u, pl.ds(halo, halo)]
        final = PAD.at[u, pl.ds(rows, halo)]
        return (
            remote(final, PAD.at[u, pl.ds(0, halo)], sh.at[u, 0], rh.at[u, 0], (g, nxt)),
            remote(first, PAD.at[u, pl.ds(halo + rows, halo)], sh.at[u, 1], rh.at[u, 1], (g, prv)),
        )

    def local_copies():
        made = [pltpu.make_async_copy(tiles_ref.at[0], T, l_sem.at[0])]
        made += [
            pltpu.make_async_copy(w_refs[j].at[0, 0], W.at[g, j], l_sem.at[1 + j]) for j in range(MATS)
        ]
        made.append(
            pltpu.make_async_copy(gain_ref.at[pl.ds(0, 1)], G.at[pl.ds(g, 1)], l_sem.at[1 + MATS])
        )
        return made

    samples_copy = pltpu.make_async_copy(samples_ref, H, l_sem.at[2 + MATS])

    barrier = pltpu.get_barrier_semaphore()
    peers = [(g, nxt), (g, prv), (g, zd), (g, cd)]
    peers += [(lax.rem(g + k, sections), d) for k in range(1, sections)]
    for peer in peers:
        pl.semaphore_signal(barrier, inc=1, device_id=peer, device_id_type=MESH)

    for copy in local_copies():
        copy.start()

    @pl.when(g == 0)
    def _():
        samples_copy.start()

    copies = local_copies()

    def outer(ref, *index):
        return jnp.concatenate([ref[*index, :halo], ref[*index, rows - halo : rows]])

    def outer_senders(u, s, n):
        v = jnp.dot(outer(H, n), W[s, 0], preferred_element_type=jnp.float32)
        v = silu(v).astype(jnp.bfloat16)
        PAD[u, halo : 2 * halo] = v[:halo]
        PAD[u, rows : rows + halo] = v[halo:]

    def inner_senders(u, s, n):
        v = jnp.dot(H[n, halo : rows - halo], W[s, 0], preferred_element_type=jnp.float32)
        PAD[u, 2 * halo : rows] = silu(v).astype(jnp.bfloat16)

    def home_senders(u, carry):
        outer_senders(u, 0, sections - 1 - u)
        inner_senders(u, 0, sections - 1 - u)
        return carry

    @pl.when(g == 0)
    def _():
        copies[1].wait()
        samples_copy.wait()
        lax.fori_loop(0, sections, home_senders, 0)

    pl.semaphore_wait(barrier, len(peers))

    @pl.when(g == 0)
    def _():
        for u in range(sections):
            for copy in halos(u):
                copy.start()

    started = {role: [] for role in roles}

    def begin(role, make, *args):
        make(*args).start()
        started[role].append((make, args))

    for role in roles[1:]:
        @pl.when(g == role)
        def _():
            for j in range(MATS if role < 3 else 2):
                for side in range(2):
                    begin(role, own, role, side, j)
            for k in range(3):
                begin(role, gain, role, k)

    copies[0].wait()
    total = blocks * domains
    base = d * blocks - HB

    def densify(b, carry):
        local = [lax.rem(source_ref[0, b, k] - base + total, total) for k in range(slots)]
        count = count_ref[0, b]
        at = pl.ds(pl.multiple_of(b * blk, blk), blk)
        for w in range(window):
            summed = jnp.zeros((blk, blk), jnp.float32)
            for k in range(slots):
                keep = ((local[k] == w) & (count > k)).astype(jnp.float32)
                summed += T[b, k].astype(jnp.float32) * keep
            E[g, at, w * blk : (w + 1) * blk] = summed.astype(jnp.bfloat16)
        return carry

    lax.fori_loop(0, blocks, densify, 0)

    for role in (1, 2):
        @pl.when(g == role)
        def _():
            for j in WHOLE_WEIGHTS[role]:
                begin(role, whole, role, j)
            for b in range(blocks):
                begin(role, own, role, role - 1, MATS + b)
                if b == 0:
                    begin(role, own, role, 2 - role, MATS)
            if not (RELAY_FIRST and role in RELAYS):
                for b in range(1, blocks):
                    begin(role, own, role, 2 - role, MATS + b)

    @pl.when(g != 0)
    def _():
        copies[1].wait()

    for copy in copies[2:]:
        copy.wait()

    def run(role, keys):
        for kind, s, j in keys:
            if kind == "x":
                forward(s, j, 0).wait_recv()
                begin(role, to_core, s, j, 0)
                if role != 0 or j not in WHOLE_WEIGHTS.get(s, ()):
                    begin(role, to_pair, s, j)
                to = weight_target(role, s, j)
                if to is not None:
                    begin(role, forward, s, j, to)
                if role == 3:
                    other = 3 - s
                    side = (other ^ role) - 1
                    if j < 2:
                        begin(role, own, role, side, j + 2)
                    if j == 3:
                        for b in BLOCK_ORDER[other]:
                            begin(role, own, role, side, MATS + b)
            elif kind == "z":
                wait_pair(s, j)
                begin(role, to_core, s, j, 1)
            elif kind == "e":
                wait_block(s, j)
                begin(role, forward, s, MATS + j, edge_target(role, s, j))
            else:
                for k in ((0, 1), (2,))[j]:
                    ref = state_part(sections - 1, k)
                    remote(ref, ref, sr.at[k], rr.at[k], (g, cd)).wait_recv()
                    begin(role, relay, k)
                if RELAY_FIRST and j == max(h for h in range(2) if RELAYS[h] == role):
                    for b in range(1, blocks):
                        begin(role, own, role, 2 - role, MATS + b)

    def poll(u, p, among):
        for role in roles:
            for (unit, piece), keys in ORDER[role].items():
                if piece == p and unit in among:
                    pl.when((g == role) & (u == unit))(functools.partial(run, role, keys))

    def wait_blocks(s, which):
        for b in which:
            passed = jnp.bool_(False)
            for role in roles:
                for section in roles[1:]:
                    if section != role and edge_target(role, section, b) is not None:
                        passed = passed | ((g == role) & (s == section))
            pl.when(jnp.logical_not(passed))(functools.partial(wait_block, s, b))

    def section_of(u):
        return jnp.maximum(u - (sections - 1), 0)

    def first_senders(u):
        s = section_of(u)

        @pl.when(s != g)
        def _():
            wait_core(s, 0)

        outer_senders(u, s, g)
        for copy in halos(u):
            copy.start()

    def inside(edges, u):
        return jnp.dot(
            edges[:, halo : halo + rows], PAD[u, halo : halo + rows], preferred_element_type=jnp.float32
        )

    def outside(edges, u):
        beside = jnp.concatenate([edges[:, :halo], edges[:, halo + rows :]], axis=1)
        read = jnp.concatenate([PAD[u, :halo], PAD[u, halo + rows :]])
        return jnp.dot(beside, read, preferred_element_type=jnp.float32)

    def update(gathered, base, s, u, state):
        mixed = base + jnp.dot(
            gathered.astype(jnp.bfloat16), W[s, 2], preferred_element_type=jnp.float32
        )
        scale = lax.rsqrt(jnp.mean(mixed * mixed, axis=-1, keepdims=True) + 1e-05)
        change = silu(mixed * scale * G[s]).astype(jnp.bfloat16)
        result = state.astype(jnp.float32) + jnp.dot(
            change, W[s, 3], preferred_element_type=jnp.float32
        )
        return result.astype(jnp.bfloat16)

    def send_state(u, parts):
        for unit in range(sections - 1):
            @pl.when((g == 0) & (u == unit))
            def _():
                for k in parts:
                    begin(0, state, sections - 1 - unit, k)

        @pl.when(u == units - 1)
        def _():
            for k in parts:
                out_copy(k).start()

    def out_copy(k):
        at = (pl.ds(0, halo), pl.ds(rows - halo, halo), pl.ds(halo, rows - 2 * halo))[k]
        return pltpu.make_async_copy(H.at[g, at], out_ref.at[0, at], so.at[k])

    every = range(units)

    def unit_body(u, carry):
        s = section_of(u)
        n = jnp.where(u < sections, sections - 1 - u, g)
        active = (u >= sections) | (g == 0)
        fetched = s != g

        poll(u, 0, (sections,))

        @pl.when(u == sections)
        def _():
            @pl.when(g != 0)
            def _():
                for k in range(2):
                    wait_state(g, k)

            first_senders(u)

        poll(u, 1, every)

        @pl.when(active)
        def _():
            @pl.when((u == sections) & (g != 0))
            def _():
                wait_state(g, 2)

            @pl.when(u >= sections)
            def _():
                inner_senders(u, s, n)

            @pl.when(fetched)
            def _():
                wait_core(s, 1)

            for i in range(2):
                at = pl.ds(i * half, half)
                BASE[at] = jnp.dot(H[n, at], W[s, 1], preferred_element_type=jnp.float32)

        poll(u, 2, every)

        @pl.when(active)
        def _():
            @pl.when(fetched)
            def _():
                wait_core(s, 2)
                wait_core(s, 3)
                wait_gain(s)
                wait_blocks(s, [*range(HB), *range(blocks - HB, blocks)])

            gathered = inside(outer(E, s), u)
            for copy in halos(u):
                copy.wait_recv()
            gathered += outside(outer(E, s), u)
            result = update(gathered, outer(BASE), s, u, outer(H, n))
            H[n, :halo] = result[:halo]
            H[n, rows - halo : rows] = result[halo:]
            send_state(u, (0, 1))

        poll(u + 1, 0, range(sections + 1, units))

        @pl.when((u >= sections) & (u < units - 1))
        def _():
            first_senders(u + 1)

        poll(u, 3, every)

        @pl.when(active)
        def _():
            @pl.when(fetched)
            def _():
                wait_blocks(s, range(HB, blocks - HB))

            at = pl.ds(halo, rows - 2 * halo)
            gathered = jnp.dot(E[s, at], PAD[u], preferred_element_type=jnp.float32)
            H[n, at] = update(gathered, BASE[at], s, u, H[n, at])
            send_state(u, (2,))
            for copy in halos(u):
                copy.wait_send()

        return carry

    lax.fori_loop(0, units, unit_body, 0)

    for role in roles:
        @pl.when(g == role)
        def _():
            run(role, ORDER[role][-1, 0])
            for make, args in started[role]:
                make(*args).wait_send()

    for k in range(3):
        out_copy(k).wait()


def shards(
    sections, domains,
    samples, w_source, w_self, w_message, w_output, norm_gain, tile_source, tile_count, tile_value,
):
    _, blocks, slots, blk, _ = tile_value.shape
    rows, width = samples.shape[1:]
    window = blocks + 2 * HB
    units = 2 * sections - 1
    chunks = MATS + blocks
    dma = pltpu.SemaphoreType.DMA
    anywhere = pl.BlockSpec(memory_space=pl.ANY)
    scalars = pl.BlockSpec(memory_space=pltpu.SMEM)
    flops = 2 * rows * width * (MATS * width + window * blk) * sections
    return pl.pallas_call(
        functools.partial(kernel, sections, domains),
        out_shape=jax.ShapeDtypeStruct((1, rows, width), jnp.bfloat16),
        in_specs=[scalars] * 2 + [anywhere] * 7,
        out_specs=anywhere,
        scratch_shapes=[
            pltpu.VMEM((sections, MATS, width, width), jnp.bfloat16),
            pltpu.VMEM((sections, rows, window * blk), jnp.bfloat16),
            pltpu.VMEM((sections, 1, width), jnp.float32),
            pltpu.VMEM((blocks, slots, blk, blk), jnp.bfloat16),
            pltpu.VMEM((sections, rows, width), jnp.bfloat16),
            pltpu.VMEM((units, window * blk, width), jnp.bfloat16),
            pltpu.VMEM((rows, width), jnp.float32),
            dma((MATS + 3,)),
            dma((sections, chunks)),
            dma((sections, MATS)),
            dma((sections, MATS, 2)),
            dma((sections,)),
            dma((3,)),
            dma((3,)),
            dma((units, 2)),
            dma((2, chunks)),
            dma((sections, chunks)),
            dma((sections, MATS)),
            dma((sections, MATS, 2)),
            dma((3,)),
            dma((sections, 3)),
            dma((3,)),
            dma((units, 2)),
            dma((3,)),
        ],
        compiler_params=pltpu.CompilerParams(
            collective_id=0, has_side_effects=True, vmem_limit_bytes=60 * 2**20
        ),
        cost_estimate=pl.CostEstimate(flops=flops, bytes_accessed=flops // 128, transcendentals=0),
    )(
        tile_source, tile_count, samples, w_source, w_self, w_message, w_output, norm_gain, tile_value
    )


def solution(mesh):
    return jax.shard_map(
        functools.partial(shards, mesh.shape["segment"], mesh.shape["dom"]),
        mesh=mesh,
        in_specs=(
            P(None, "dom", None),
            P("segment", None, None, None),
            P("segment", None, None, None),
            P("segment", None, None, None),
            P("segment", None, None, None),
            P("segment", None, None),
            P("segment", "dom", None),
            P("segment", "dom"),
            P("segment", "dom", None, None, None),
        ),
        out_specs=P("segment", "dom", None),
        check_vma=False,
    )
```

```python
import functools

import jax
import jax.numpy as jnp
from jax import lax
from jax.experimental import pallas as pl
from jax.experimental.pallas import tpu as pltpu
from jax.sharding import PartitionSpec as P

HB = 1
MESH = pl.DeviceIdType.MESH
MATS = 4

EDGES_BY_LAST = {1: [0, 1], 2: []}
WEIGHTS_BY_FIRST = {1: [0, 3], 2: []}
WHOLE_WEIGHTS = {1: [], 2: [0, 1, 3]}
BLOCKS_BY_ONE = 2
BLOCK_ORDER = {2: [1, 3, 2, 0], 1: [1, 2, 0, 3]}
RELAYS = (1, 2)
WEIGHTS_BY_TWO = []
RELAY_FIRST = True
ORDER = {
    0: {
        (0, 2): [('x', 1, 0), ('x', 1, 1)],
        (1, 3): [('x', 1, 2)],
        (2, 1): [('x', 1, 3)],
        (2, 2): [('x', 2, 3)],
        (3, 1): [('z', 2, 0)],
        (4, 0): [('z', 1, 0), ('x', 2, 1)],
        (4, 1): [('z', 2, 1), ('x', 2, 0), ('x', 2, 2), ('z', 2, 3), ('z', 1, 2), ('z', 1, 1)],
        (4, 2): [('e', 2, 0), ('z', 1, 3), ('e', 1, 3)],
        (4, 3): [('x', 3, 0), ('z', 2, 2), ('e', 2, 2), ('x', 3, 1), ('e', 1, 2)],
        (5, 1): [('e', 2, 3), ('e', 2, 1), ('x', 3, 2)],
        (5, 2): [('z', 3, 0)],
        (6, 0): [('x', 3, 3)],
        (6, 1): [('z', 3, 1)],
        (6, 2): [('z', 3, 2), ('z', 3, 3)],
        (-1, 0): [],
    },
    1: {
        (4, 0): [('x', 3, 0), ('x', 2, 0), ('z', 3, 0), ('x', 3, 1), ('r', 3, 0), ('z', 3, 1), ('x', 3, 2), ('x', 2, 2), ('z', 2, 2), ('z', 3, 2)],
        (4, 1): [('x', 2, 1), ('x', 3, 3), ('e', 3, 1)],
        (4, 2): [('x', 2, 3), ('z', 2, 0)],
        (5, 0): [('z', 3, 3)],
        (5, 1): [('e', 3, 0), ('z', 2, 1)],
        (5, 2): [('z', 2, 3)],
        (-1, 0): [],
    },
    2: {
        (4, 0): [('x', 3, 1), ('x', 3, 2), ('x', 3, 0), ('z', 3, 1), ('x', 1, 1), ('z', 3, 2), ('x', 1, 0), ('r', 3, 1), ('x', 1, 2), ('x', 3, 3), ('z', 1, 1), ('z', 1, 0)],
        (4, 2): [('z', 1, 2), ('z', 3, 3), ('e', 3, 3), ('x', 1, 3), ('z', 1, 3), ('z', 3, 0), ('e', 3, 2)],
        (-1, 0): [],
    },
    3: {
        (4, 0): [('x', 1, 0), ('x', 2, 0), ('x', 1, 1), ('x', 1, 2), ('x', 2, 2), ('x', 2, 1), ('x', 2, 3), ('z', 1, 1), ('e', 1, 0), ('z', 2, 0), ('x', 1, 3), ('z', 1, 0)],
        (4, 2): [('z', 1, 2), ('e', 1, 1), ('z', 1, 3), ('z', 2, 1), ('z', 2, 2)],
        (5, 1): [('z', 2, 3)],
        (-1, 0): [],
    },
}


def edge_target(role, section, block):
    if section in EDGES_BY_LAST and role in (0, 3):
        if (block in EDGES_BY_LAST[section]) == (role == 3):
            return 3 - section
    if section == 3 and role == (1 if block < BLOCKS_BY_ONE else 2):
        return 0
    return None


def weight_target(role, section, j):
    if section in WEIGHTS_BY_FIRST and role in (0, 3):
        if (j in WEIGHTS_BY_FIRST[section]) == (role == 0):
            return 3 - section
    if section == 3 and role == (2 if j in WEIGHTS_BY_TWO else 1):
        return 0
    return None


def silu(v):
    half = 0.5 * v
    return half + half * jnp.tanh(half)


def kernel(
    sections, domains,
    source_ref, count_ref, samples_ref, wa_ref, wb_ref, wc_ref, wd_ref, gain_ref, tiles_ref,
    out_ref,
    W, E, G, T, H, PAD, BASE,
    l_sem, rx, rz, rc, rg, ra, rr, rh, sx, sf, sz, sc, sg, sa, sr, sh, so,
):
    g = lax.axis_index("segment")
    d = lax.axis_index("dom")
    w_refs = (wa_ref, wb_ref, wc_ref, wd_ref)
    _, blocks, slots, blk, _ = tiles_ref.shape
    window = blocks + 2 * HB
    rows = blocks * blk
    halo = HB * blk
    width = samples_ref.shape[-1]
    quarter = width // 4
    half = rows // 2
    per_half = blocks // 2
    units = 2 * sections - 1
    roles = range(sections)
    q = lax.rem(d, 4)
    zd = d + 2 - 4 * (q // 2)
    cd = d + 1 - 2 * lax.rem(d, 2)
    nxt, prv = lax.rem(d + 1, domains), lax.rem(d + domains - 1, domains)
    zq = lax.rem(zd, 4)
    cq = lax.rem(cd, 4)
    czq = lax.rem(q + 1 - 2 * lax.rem(q, 2) + 2, 4)

    def part(index):
        return pl.ds(pl.multiple_of(index * quarter, quarter), quarter)

    def remote(src, dst, send, recv, device):
        return pltpu.make_async_remote_copy(
            src_ref=src, dst_ref=dst, send_sem=send, recv_sem=recv,
            device_id=device, device_id_type=MESH,
        )

    def piece_of(s, j):
        if j < MATS:
            return W.at[s, j, part(q)]
        return E.at[s, pl.ds((j - MATS) * blk, blk)]

    def own(role, side, j):
        src = w_refs[j].at[0, 0, part(q)] if j < MATS else piece_of(role, j)
        to = role ^ (1 + side)
        return remote(src, piece_of(role, j), sx.at[side, j], rx.at[role, j], (to, d))

    def forward(s, j, to):
        return remote(piece_of(s, j), piece_of(s, j), sf.at[s, j], rx.at[s, j], (to, d))

    def to_pair(s, j):
        return remote(W.at[s, j, part(q)], W.at[s, j, part(q)], sz.at[s, j], rz.at[s, j], (g, zd))

    def to_core(s, j, kind):
        at = part(zq if kind else q)
        return remote(W.at[s, j, at], W.at[s, j, at], sc.at[s, j, kind], rc.at[s, j, kind], (g, cd))

    def wait_pair(s, j):
        remote(W.at[s, j, part(zq)], W.at[s, j, part(zq)], sz.at[s, j], rz.at[s, j], (g, zd)).wait_recv()

    def wait_core(s, j):
        for kind, index in enumerate((cq, czq)):
            at = part(index)
            remote(W.at[s, j, at], W.at[s, j, at], sc.at[s, j, kind], rc.at[s, j, kind], (g, cd)).wait_recv()

    def wait_block(s, b):
        at = pl.ds(b * blk, blk)
        remote(E.at[s, at], E.at[s, at], sf.at[s, MATS + b], rx.at[s, MATS + b], (g, cd)).wait_recv()

    def gain(role, k):
        to = role ^ (1 + k)
        return remote(gain_ref.at[pl.ds(0, 1)], G.at[pl.ds(role, 1)], sg.at[k], rg.at[role], (to, d))

    def wait_gain(s):
        remote(gain_ref.at[pl.ds(0, 1)], G.at[pl.ds(s, 1)], sg.at[0], rg.at[s], (g, cd)).wait_recv()

    def state_part(n, k):
        at = (pl.ds(0, halo), pl.ds(rows - halo, halo), pl.ds(halo, rows - 2 * halo))[k]
        return H.at[n, at]

    def state(n, k):
        last = sections - 1
        ref = state_part(n, k)
        if n == last:
            return remote(ref, ref, sa.at[n, k], rr.at[k], (RELAYS[k // 2], d))
        return remote(ref, ref, sa.at[n, k], ra.at[k], (n, d))

    def relay(k):
        last = sections - 1
        ref = state_part(last, k)
        return remote(ref, ref, sr.at[k], ra.at[k], (last, d))

    def wait_state(n, k):
        ref = state_part(n, k)
        remote(ref, ref, sr.at[k], ra.at[k], (g, cd)).wait_recv()

    def whole(role, j):
        at = part(zq)
        src = w_refs[j].at[0, 0, at]
        return remote(src, W.at[role, j, at], sz.at[role, j], rz.at[role, j], (0, d))

    def halos(u):
        first = PAD.at[u, pl.ds(halo, halo)]
        final = PAD.at[u, pl.ds(rows, halo)]
        return (
            remote(final, PAD.at[u, pl.ds(0, halo)], sh.at[u, 0], rh.at[u, 0], (g, nxt)),
            remote(first, PAD.at[u, pl.ds(halo + rows, halo)], sh.at[u, 1], rh.at[u, 1], (g, prv)),
        )

    def local_copies():
        made = [pltpu.make_async_copy(tiles_ref.at[0], T, l_sem.at[0])]
        made += [
            pltpu.make_async_copy(w_refs[j].at[0, 0], W.at[g, j], l_sem.at[1 + j]) for j in range(MATS)
        ]
        made.append(
            pltpu.make_async_copy(gain_ref.at[pl.ds(0, 1)], G.at[pl.ds(g, 1)], l_sem.at[1 + MATS])
        )
        return made

    samples_copy = pltpu.make_async_copy(samples_ref, H, l_sem.at[2 + MATS])

    barrier = pltpu.get_barrier_semaphore()
    peers = [(g, nxt), (g, prv), (g, zd), (g, cd)]
    peers += [(lax.rem(g + k, sections), d) for k in range(1, sections)]
    for peer in peers:
        pl.semaphore_signal(barrier, inc=1, device_id=peer, device_id_type=MESH)

    for copy in local_copies():
        copy.start()

    @pl.when(g == 0)
    def _():
        samples_copy.start()

    copies = local_copies()

    def outer(ref, *index):
        return jnp.concatenate([ref[*index, :halo], ref[*index, rows - halo : rows]])

    def outer_senders(u, s, n):
        v = jnp.dot(outer(H, n), W[s, 0], preferred_element_type=jnp.float32)
        v = silu(v).astype(jnp.bfloat16)
        PAD[u, halo : 2 * halo] = v[:halo]
        PAD[u, rows : rows + halo] = v[halo:]

    def inner_senders(u, s, n):
        v = jnp.dot(H[n, halo : rows - halo], W[s, 0], preferred_element_type=jnp.float32)
        PAD[u, 2 * halo : rows] = silu(v).astype(jnp.bfloat16)

    def home_senders(u, carry):
        outer_senders(u, 0, sections - 1 - u)
        inner_senders(u, 0, sections - 1 - u)
        return carry

    @pl.when(g == 0)
    def _():
        copies[1].wait()
        samples_copy.wait()
        lax.fori_loop(0, sections, home_senders, 0)

    pl.semaphore_wait(barrier, len(peers))

    @pl.when(g == 0)
    def _():
        for u in range(sections):
            for copy in halos(u)[::-1]:
                copy.start()

    started = {role: [] for role in roles}

    def begin(role, make, *args):
        make(*args).start()
        started[role].append((make, args))

    for role in roles[1:]:
        @pl.when(g == role)
        def _():
            for j in range(MATS if role < 3 else 2):
                for side in range(2):
                    begin(role, own, role, side, j)
            for k in range(3):
                begin(role, gain, role, k)

    copies[0].wait()
    total = blocks * domains
    base = d * blocks - HB

    def densify(b, carry):
        local = [lax.rem(source_ref[0, b, k] - base + total, total) for k in range(slots)]
        count = count_ref[0, b]
        at = pl.ds(pl.multiple_of(b * blk, blk), blk)
        for w in range(window):
            summed = jnp.zeros((blk, blk), jnp.float32)
            for k in range(slots):
                keep = ((local[k] == w) & (count > k)).astype(jnp.float32)
                summed += T[b, k].astype(jnp.float32) * keep
            E[g, at, w * blk : (w + 1) * blk] = summed.astype(jnp.bfloat16)
        return carry

    lax.fori_loop(0, blocks, densify, 0)

    for role in (1, 2):
        @pl.when(g == role)
        def _():
            for j in WHOLE_WEIGHTS[role]:
                begin(role, whole, role, j)
            for b in range(blocks):
                begin(role, own, role, role - 1, MATS + b)
                if b == 0:
                    begin(role, own, role, 2 - role, MATS)
            if not (RELAY_FIRST and role in RELAYS):
                for b in range(1, blocks):
                    begin(role, own, role, 2 - role, MATS + b)

    @pl.when(g != 0)
    def _():
        copies[1].wait()

    for copy in copies[2:]:
        copy.wait()

    def run(role, keys):
        for kind, s, j in keys:
            if kind == "x":
                forward(s, j, 0).wait_recv()
                begin(role, to_core, s, j, 0)
                if role != 0 or j not in WHOLE_WEIGHTS.get(s, ()):
                    begin(role, to_pair, s, j)
                to = weight_target(role, s, j)
                if to is not None:
                    begin(role, forward, s, j, to)
                if role == 3:
                    other = 3 - s
                    side = (other ^ role) - 1
                    if j < 2:
                        begin(role, own, role, side, j + 2)
                    if j == 3:
                        for b in BLOCK_ORDER[other]:
                            begin(role, own, role, side, MATS + b)
            elif kind == "z":
                wait_pair(s, j)
                begin(role, to_core, s, j, 1)
            elif kind == "e":
                wait_block(s, j)
                begin(role, forward, s, MATS + j, edge_target(role, s, j))
            else:
                for k in ((0, 1), (2,))[j]:
                    ref = state_part(sections - 1, k)
                    remote(ref, ref, sr.at[k], rr.at[k], (g, cd)).wait_recv()
                    begin(role, relay, k)
                if RELAY_FIRST and j == max(h for h in range(2) if RELAYS[h] == role):
                    for b in range(1, blocks):
                        begin(role, own, role, 2 - role, MATS + b)

    def poll(u, p, among):
        for role in roles:
            for (unit, piece), keys in ORDER[role].items():
                if piece == p and unit in among:
                    pl.when((g == role) & (u == unit))(functools.partial(run, role, keys))

    def wait_blocks(s, which):
        for b in which:
            passed = jnp.bool_(False)
            for role in roles:
                for section in roles[1:]:
                    if section != role and edge_target(role, section, b) is not None:
                        passed = passed | ((g == role) & (s == section))
            pl.when(jnp.logical_not(passed))(functools.partial(wait_block, s, b))

    def section_of(u):
        return jnp.maximum(u - (sections - 1), 0)

    def first_senders(u):
        s = section_of(u)

        @pl.when(s != g)
        def _():
            wait_core(s, 0)

        outer_senders(u, s, g)
        for copy in halos(u):
            copy.start()

    def inside(edges, u):
        return jnp.dot(
            edges[:, halo : halo + rows], PAD[u, halo : halo + rows], preferred_element_type=jnp.float32
        )

    def outside(edges, u):
        beside = jnp.concatenate([edges[:, :halo], edges[:, halo + rows :]], axis=1)
        read = jnp.concatenate([PAD[u, :halo], PAD[u, halo + rows :]])
        return jnp.dot(beside, read, preferred_element_type=jnp.float32)

    def update(gathered, base, s, u, state):
        mixed = base + jnp.dot(
            gathered.astype(jnp.bfloat16), W[s, 2], preferred_element_type=jnp.float32
        )
        scale = lax.rsqrt(jnp.mean(mixed * mixed, axis=-1, keepdims=True) + 1e-05)
        change = silu(mixed * scale * G[s]).astype(jnp.bfloat16)
        result = state.astype(jnp.float32) + jnp.dot(
            change, W[s, 3], preferred_element_type=jnp.float32
        )
        return result.astype(jnp.bfloat16)

    def send_state(u, parts):
        for unit in range(sections - 1):
            @pl.when((g == 0) & (u == unit))
            def _():
                for k in parts:
                    begin(0, state, sections - 1 - unit, k)

        @pl.when(u == units - 1)
        def _():
            for k in parts:
                out_copy(k).start()

    def out_copy(k):
        at = (pl.ds(0, halo), pl.ds(rows - halo, halo), pl.ds(halo, rows - 2 * halo))[k]
        return pltpu.make_async_copy(H.at[g, at], out_ref.at[0, at], so.at[k])

    every = range(units)

    def unit_body(u, carry):
        s = section_of(u)
        n = jnp.where(u < sections, sections - 1 - u, g)
        active = (u >= sections) | (g == 0)
        fetched = s != g

        poll(u, 0, (sections,))

        @pl.when(u == sections)
        def _():
            @pl.when(g != 0)
            def _():
                for k in range(2):
                    wait_state(g, k)

            first_senders(u)

        poll(u, 1, every)

        @pl.when(active)
        def _():
            @pl.when((u == sections) & (g != 0))
            def _():
                wait_state(g, 2)

            @pl.when(u >= sections)
            def _():
                inner_senders(u, s, n)

            @pl.when(fetched)
            def _():
                wait_core(s, 1)

            for i in range(2):
                at = pl.ds(i * half, half)
                BASE[at] = jnp.dot(H[n, at], W[s, 1], preferred_element_type=jnp.float32)

        poll(u, 2, every)

        @pl.when(active)
        def _():
            @pl.when(fetched)
            def _():
                wait_core(s, 2)
                wait_core(s, 3)
                wait_gain(s)
                wait_blocks(s, [*range(HB), *range(blocks - HB, blocks)])

            gathered = inside(outer(E, s), u)
            for copy in halos(u):
                copy.wait_recv()
            gathered += outside(outer(E, s), u)
            result = update(gathered, outer(BASE), s, u, outer(H, n))
            H[n, :halo] = result[:halo]
            H[n, rows - halo : rows] = result[halo:]
            send_state(u, (0, 1))

        poll(u + 1, 0, range(sections + 1, units))

        @pl.when((u >= sections) & (u < units - 1))
        def _():
            first_senders(u + 1)

        poll(u, 3, every)

        @pl.when(active)
        def _():
            @pl.when(fetched)
            def _():
                wait_blocks(s, range(HB, blocks - HB))

            at = pl.ds(halo, rows - 2 * halo)
            gathered = jnp.dot(E[s, at], PAD[u], preferred_element_type=jnp.float32)
            H[n, at] = update(gathered, BASE[at], s, u, H[n, at])
            send_state(u, (2,))
            for copy in halos(u):
                copy.wait_send()

        return carry

    lax.fori_loop(0, units, unit_body, 0)

    for role in roles:
        @pl.when(g == role)
        def _():
            run(role, ORDER[role][-1, 0])
            for make, args in started[role]:
                make(*args).wait_send()

    for k in range(3):
        out_copy(k).wait()


def shards(
    sections, domains,
    samples, w_source, w_self, w_message, w_output, norm_gain, tile_source, tile_count, tile_value,
):
    _, blocks, slots, blk, _ = tile_value.shape
    rows, width = samples.shape[1:]
    window = blocks + 2 * HB
    units = 2 * sections - 1
    chunks = MATS + blocks
    dma = pltpu.SemaphoreType.DMA
    anywhere = pl.BlockSpec(memory_space=pl.ANY)
    scalars = pl.BlockSpec(memory_space=pltpu.SMEM)
    flops = 2 * rows * width * (MATS * width + window * blk) * sections
    return pl.pallas_call(
        functools.partial(kernel, sections, domains),
        out_shape=jax.ShapeDtypeStruct((1, rows, width), jnp.bfloat16),
        in_specs=[scalars] * 2 + [anywhere] * 7,
        out_specs=anywhere,
        scratch_shapes=[
            pltpu.VMEM((sections, MATS, width, width), jnp.bfloat16),
            pltpu.VMEM((sections, rows, window * blk), jnp.bfloat16),
            pltpu.VMEM((sections, 1, width), jnp.float32),
            pltpu.VMEM((blocks, slots, blk, blk), jnp.bfloat16),
            pltpu.VMEM((sections, rows, width), jnp.bfloat16),
            pltpu.VMEM((units, window * blk, width), jnp.bfloat16),
            pltpu.VMEM((rows, width), jnp.float32),
            dma((MATS + 3,)),
            dma((sections, chunks)),
            dma((sections, MATS)),
            dma((sections, MATS, 2)),
            dma((sections,)),
            dma((3,)),
            dma((3,)),
            dma((units, 2)),
            dma((2, chunks)),
            dma((sections, chunks)),
            dma((sections, MATS)),
            dma((sections, MATS, 2)),
            dma((3,)),
            dma((sections, 3)),
            dma((3,)),
            dma((units, 2)),
            dma((3,)),
        ],
        compiler_params=pltpu.CompilerParams(
            collective_id=0, has_side_effects=True, vmem_limit_bytes=60 * 2**20
        ),
        cost_estimate=pl.CostEstimate(flops=flops, bytes_accessed=flops // 128, transcendentals=0),
    )(
        tile_source, tile_count, samples, w_source, w_self, w_message, w_output, norm_gain, tile_value
    )


def solution(mesh):
    return jax.shard_map(
        functools.partial(shards, mesh.shape["segment"], mesh.shape["dom"]),
        mesh=mesh,
        in_specs=(
            P(None, "dom", None),
            P("segment", None, None, None),
            P("segment", None, None, None),
            P("segment", None, None, None),
            P("segment", None, None, None),
            P("segment", None, None),
            P("segment", "dom", None),
            P("segment", "dom"),
            P("segment", "dom", None, None, None),
        ),
        out_specs=P("segment", "dom", None),
        check_vma=False,
    )
```
